32 devices in a mesh: cuts: 2 (over x), mode: 16 (over z, y, core).
Axes of the slice: x: 2, y: 2, z: 4, core: 2. Of those that a mesh axis runs over, the one named last changes fastest.
Arguments:
- stem_tensor: float32 [2, 2, 16, 512, 512], P(None, 'cuts', 'mode'), parts along dimension 1, may hold values from -6 to 6
- branch_tensors: float32 [4, 2, 512, 512], replicated, may hold values from -0.1875 to 0.1875
- branch_order: int32 [4], replicated, may hold values from 0 to 3, each once
Outputs:
- new_stem: float32 [2, 2, 16, 512, 512], P(None, 'cuts', 'mode'), parts along dimension 1
The draws below stay inside these ranges and needn't reach their ends.
There are 2 independent parts, one for each index of `cuts`. The reference program is written for one: setup_inputs(seed, part) draws one part's arguments, and reference() takes and returns one part's arrays. A program takes and returns all parts, laid end to end along the dimension named above; an argument that names none is the same for every part. Nothing has to cross between parts.
Inputs may be any that keep to these rules, and one draw needn't show every extreme that they name: `branch_order`: a permutation of the 4 branch tensors.
All inputs are finite; a program needn't handle non-finite values.
Results may differ from the reference program's by a relative error of at most 0.00007.
Values sent between devices are 32-bit elements; how exact they have to be, the bound alone decides.
A program may use at most 64 MiB of HBM per device.

```python
import jax
import jax.numpy as jnp
from jax import lax

BW = 512
NB = 4
SL = 1
GRID = 16
N_MODE = 16


def level_of(stream_key, shape, shards, smallest, high):
    def one(position, parts):
        heights = jax.random.uniform(jax.random.fold_in(jax.random.fold_in(stream_key, 6), position), (parts,), jnp.float32, smallest / len(shards), high / len(shards))
        return jnp.repeat(jnp.exp(heights), shape[position] // parts).reshape((-1,) + (1,) * (len(shape) - position - 1))

    factor_of = one(*shards[0])
    for cut in shards[1:]:
        factor_of = factor_of * one(*cut)
    return factor_of


def noise(key, shape, scale, most, pieces=(), dtype=jnp.bfloat16):
    array = jax.random.normal(key, shape, jnp.float32) * scale
    if len(pieces) > 0:
        array = level_of(key, shape, pieces, -0.22, 0.18) * array
    return jnp.clip(array, min=-most, max=most).astype(dtype)


def setup_inputs(seed: int = 0, part: int = 0) -> dict:
    seeds = jax.random.split(jax.random.key(seed), 4)
    part_splits = jax.random.split(jax.random.fold_in(seeds[3], part), 4)
    stem_tensor = noise(part_splits[0], (2, SL, GRID, BW, BW), 1.0, 6.0, ((2, 16),), jnp.float32)
    branch_tensors = noise(seeds[1], (NB, 2, BW, BW), (2 * BW) ** -0.5, 0.1875, (), jnp.float32)
    branch_order = jax.random.permutation(seeds[2], NB).astype(jnp.int32)
    return dict(stem_tensor=stem_tensor, branch_tensors=branch_tensors, branch_order=branch_order)


def complex_product(first, second, form):
    high = lax.Precision.HIGHEST
    real = jnp.einsum(form, first[0], second[0], precision=high) - jnp.einsum(form, first[1], second[1], precision=high)
    imag = jnp.einsum(form, first[0], second[1], precision=high) + jnp.einsum(form, first[1], second[0], precision=high)
    return jnp.stack([real, imag])


def reference(stem_tensor, branch_tensors, branch_order):
    branches = [branch_tensors[branch_order[index]] for index in range(NB)]
    field = complex_product(stem_tensor, branches[0], 'sgce,cd->sgde')
    field = complex_product(field, branches[1], 'sgce,ed->sgcd')
    split = field.reshape(2, SL, N_MODE, N_MODE, BW // N_MODE, BW)
    split = jnp.swapaxes(split, 2, 3).reshape(2, SL, N_MODE, BW, BW)
    field = complex_product(split, branches[2], 'sgce,cd->sgde')
    return complex_product(field, branches[3], 'sgce,ed->sgcd')
```

```python
import functools

import jax
import jax.numpy as jnp
from jax import lax
from jax.experimental import pallas as pl
from jax.experimental.pallas import tpu as pltpu
from jax.sharding import PartitionSpec as P

MESH = pl.DeviceIdType.MESH
LANES = 128
F32, BF16 = jnp.float32, jnp.bfloat16


def flip(value, mask, size):
    result, bit = 0, 1
    while bit < size:
        digit = lax.rem(lax.div(value, bit), 2)
        result = result + (1 - digit if (mask // bit) % 2 else digit) * bit
        bit *= 2
    return result


def split(value):
    high = value.astype(BF16)
    return high, (value - high.astype(F32)).astype(BF16)


def dot(a, b):
    return jnp.dot(a, b, preferred_element_type=F32)


def dot3(high, low, right_high, right_low):
    return dot(high, right_high) + (dot(high, right_low) + dot(low, right_high))


def complex_rows(rows, right_high, right_low):
    m = rows.shape[0] // 2
    high, low = split(rows)
    by_real = dot3(high, low, right_high[0], right_low[0])
    by_imag = dot3(high, low, right_high[1], right_low[1])
    return by_real[:m] - by_imag[m:], by_imag[:m] + by_real[m:]


def kernel(n, order_ref, stem_ref, branch_ref, out_ref, stem, xh, xl, bh, bl, dh, dl, wh, wl,
           lch, lcl, lct, sent, got, order, order_sem, stem_sem, left_sem, branch_sem, send_sem, recv_sem, left_0, left_1, *branch):
    bw = stem.shape[1]
    rows = bw // n
    per = LANES // rows
    groups = n // per
    me = lax.axis_index("mode")
    z, q = lax.div(me, per), lax.rem(me, per)
    sequence = [groups // 2] + [s for s in range(1, groups) if s != groups // 2] + [0]
    early = sequence[: groups // 2]

    def column(s):
        return pl.ds(pl.multiple_of(flip(z, s, groups) * LANES, LANES), LANES)

    barrier = pltpu.get_barrier_semaphore()
    for k in range(n - 1, 0, -1):
        pl.semaphore_signal(barrier, inc=1, device_id={"mode": flip(me, k, n)}, device_id_type=MESH)

    order_copy = pltpu.make_async_copy(order_ref, order, order_sem)
    order_copy.start()
    halves = [pl.ds(h * (bw // 2), bw // 2) for h in range(2)]
    lead = sequence[0]
    left, left_copies, stem_copies = (left_0, left_1), [], []
    for h, half in enumerate(halves):
        left_copies.append(pltpu.make_async_copy(
            branch_ref.at[:, :, half, column(lead)], left[h], left_sem.at[h]))
        stem_copies.append([
            pltpu.make_async_copy(stem_ref.at[part, half], stem.at[part, half], stem_sem.at[part, h]) for part in range(2)])
        for copy in [left_copies[h]] + stem_copies[h]:
            copy.start()
    branch_copies = {
        s: pltpu.make_async_copy(branch_ref.at[:, :, :, column(s)], branch[s], branch_sem.at[s]) for s in sequence}
    order_copy.wait()
    o0, o1, o2, o3 = (order[k] for k in range(4))

    def left_rows(s):
        return jnp.concatenate([branch[s][o0, part].T for part in range(2)], axis=0)

    def first_rows(s):
        return complex_rows(left_rows(s), xh, xl)

    def hop(s, k):
        j = flip(q, k, per)
        return pltpu.make_async_remote_copy(
            src_ref=sent.at[s, j], dst_ref=got.at[s, q], send_sem=send_sem.at[s, k], recv_sem=recv_sem.at[s, q],
            device_id={"mode": flip(z, s, groups) * per + j}, device_id_type=MESH)

    def own(s):
        return pltpu.make_async_copy(sent.at[s, q], got.at[s, q], recv_sem.at[s, q])

    def send(s, real, imag):
        for j in range(per):
            sent[s, j, 0] = real[j * rows:(j + 1) * rows]
            sent[s, j, 1] = imag[j * rows:(j + 1) * rows]
        for k in range(per):
            own(s).start() if s == 0 and k == 0 else hop(s, k).start()

    by = [None, None]
    for h, half in enumerate(halves):
        left_copies[h].wait()
        high, low = split(jnp.concatenate([left[h][o0, part].T for part in range(2)], axis=0))
        for part in range(2):
            stem_copies[h][part].wait()
            if h == part == 1:
                for s in sequence[1:] + [lead]:
                    branch_copies[s].start()
            xh[part, half], xl[part, half] = split(stem[part, half])
            add = dot3(high, low, xh[part, half], xl[part, half])
            by[part] = add if h == 0 else by[part] + add
    real, imag = by[0][:LANES] - by[1][LANES:], by[1][:LANES] + by[0][LANES:]
    pl.semaphore_wait(barrier, n - 1)
    send(lead, real, imag)
    for s in early[1:]:
        branch_copies[s].wait()
        send(s, *first_rows(s))
    for s in sequence[len(early):] + [lead]:
        branch_copies[s].wait()

    for s in range(groups):
        for part in range(2):
            bh[part, :, column(s)], bl[part, :, column(s)] = split(branch[s][o1, part])
            dh[part, :, column(s)], dl[part, :, column(s)] = split(branch[s][o3, part])

    def both(i, carry):
        at = pl.ds(pl.multiple_of(i * LANES, LANES), LANES)
        high = jnp.concatenate([bh[0, at], bh[1, at]], axis=0)
        low = jnp.concatenate([bl[0, at], bl[1, at]], axis=0)
        by_real = dot3(high, low, dh[0], dl[0])
        by_imag = dot3(high, low, dh[1], dl[1])
        wh[0, at], wl[0, at] = split(by_real[:LANES] - by_imag[LANES:])
        wh[1, at], wl[1, at] = split(by_imag[:LANES] + by_real[LANES:])
        return carry

    lax.fori_loop(0, bw // LANES, both, 0)

    for s in sequence[len(early):]:
        real, imag = first_rows(s)
        send(s, *complex_rows(jnp.concatenate([real, imag], axis=0), wh, wl))

    last = sequence[-2]

    def third_rows(t, part, s):
        if s != last:
            return branch[t][o2, part, column(s), :]
        base = flip(z, s, groups) * LANES
        return jnp.concatenate([
            branch[t][o2, part, pl.ds(pl.multiple_of(base + flip(q, k, per) * rows, rows), rows), :]
            for k in range(per)], axis=0)

    for s in range(groups):
        for t in range(groups):
            real, imag = (split(third_rows(t, part, s).T) for part in range(2))
            top = column(t)
            low_half = pl.ds(pl.multiple_of(bw + flip(z, t, groups) * LANES, LANES), LANES)
            for ref, r, i in ((lch, real[0], imag[0]), (lcl, real[1], imag[1])):
                ref[s, top, :LANES] = r
                ref[s, top, LANES:] = -i
                ref[s, low_half, :LANES] = i
                ref[s, low_half, LANES:] = r
            if s == last:
                tail = slice(LANES - rows, LANES)
                for place, (r, i) in enumerate(((real[0], imag[0]), (real[0], imag[0]), (real[1], imag[1]))):
                    at = slice(2 * place * rows, (2 * place + 1) * rows)
                    after = slice((2 * place + 1) * rows, (2 * place + 2) * rows)
                    lct[top, at] = r[:, tail]
                    lct[top, after] = -i[:, tail]
                    lct[low_half, at] = i[:, tail]
                    lct[low_half, after] = r[:, tail]

    arrivals = [0] + [s for s in early if s != groups // 2] + [groups // 2] + [s for s in sequence[len(early):] if s]
    tile = 2 * LANES

    def arrive(s, j):
        pltpu.make_async_copy(got.at[s, j], got.at[s, j], recv_sem.at[s, j]).wait()

    def result(i):
        part, row = divmod(i * tile, bw)
        return part, slice(row, row + tile)

    for index, s in enumerate(arrivals):
        places = [flip(q, k, per) if s == last else k for k in range(per)]
        if s == last:
            final = places.pop()
        for j in places:
            arrive(s, j)
        blank = [jnp.zeros((rows, bw), F32)] * (per - len(places))
        arrived = jnp.concatenate([piece for part in range(2) for piece in [got[s, j, part] for j in places] + blank], axis=0)
        if s in early:
            arrived = jnp.concatenate(complex_rows(arrived, wh, wl), axis=0)
        right_high, right_low = split(arrived)
        for i in range(2 * bw // tile):
            at = slice(i * tile, (i + 1) * tile)
            add = dot3(lch[s, at], lcl[s, at], right_high, right_low)
            out_ref[result(i)] = add if index == 0 else out_ref[result(i)] + add
    arrive(last, final)
    high, low = split(jnp.concatenate([got[last, final, 0], got[last, final, 1]], axis=0))
    right = jnp.concatenate([high, low, high], axis=0)
    for i in range(2 * bw // tile):
        at = slice(i * tile, (i + 1) * tile)
        out_ref[result(i)] = out_ref[result(i)] + dot(lct[at, : 6 * rows], right)
    for s in range(groups):
        for k in range(per):
            if s or k:
                hop(s, k).wait_send()


def fused(n, stem_tensor, branch_tensors, branch_order):
    bw = stem_tensor.shape[-1]
    rows = bw // n
    per = LANES // rows
    groups = n // per
    square = pltpu.VMEM((2, bw, bw), BF16)
    hbm = functools.partial(pltpu.with_memory_space_constraint, memory_space=pltpu.HBM)
    window = pltpu.VMEM((groups, 2 * bw, 2 * LANES), BF16)
    return pl.pallas_call(
        functools.partial(kernel, n),
        out_shape=jax.ShapeDtypeStruct((2, bw, bw), F32),
        in_specs=[pl.BlockSpec(memory_space=pl.ANY)] * 3,
        out_specs=pl.BlockSpec(memory_space=pltpu.VMEM),
        scratch_shapes=[
            pltpu.VMEM((2, bw, bw), F32),
            *[square] * 8,
            window,
            window,
            pltpu.VMEM((2 * bw, 2 * LANES), BF16),
            pltpu.VMEM((groups, per, 2, rows, bw), F32),
            pltpu.VMEM((groups, per, 2, rows, bw), F32),
            pltpu.SMEM(branch_order.shape, jnp.int32),
            pltpu.SemaphoreType.DMA,
            pltpu.SemaphoreType.DMA((2, 2)),
            pltpu.SemaphoreType.DMA((2,)),
            pltpu.SemaphoreType.DMA((groups,)),
            pltpu.SemaphoreType.DMA((groups, per)),
            pltpu.SemaphoreType.DMA((groups, per)),
            *[pltpu.VMEM((4, 2, bw // 2, LANES), F32)] * 2,
            *[pltpu.VMEM((4, 2, bw, LANES), F32)] * groups,
        ],
        compiler_params=pltpu.CompilerParams(collective_id=0, has_side_effects=True, vmem_limit_bytes=40 << 20),
    )(hbm(branch_order), hbm(stem_tensor.reshape(2, bw, bw)), hbm(branch_tensors)).reshape(stem_tensor.shape)


def complex_product(first, second, form):
    high = lax.Precision.HIGHEST
    real = jnp.einsum(form, first[0], second[0], precision=high) - jnp.einsum(form, first[1], second[1], precision=high)
    imag = jnp.einsum(form, first[0], second[1], precision=high) + jnp.einsum(form, first[1], second[0], precision=high)
    return jnp.stack([real, imag])


def plain(stem_tensor, branch_tensors, branch_order):
    field = stem_tensor[:, :, 0]
    chosen = [branch_tensors[branch_order[index]] for index in range(4)]
    field = complex_product(field, chosen[0], "sce,cd->sde")
    field = complex_product(field, chosen[1], "sce,ed->scd")
    moved = lax.all_to_all(field[:, :, None], "mode", split_axis=3, concat_axis=2, tiled=True)
    merged = moved.reshape(field.shape)
    merged = complex_product(merged, chosen[2], "sce,cd->sde")
    return complex_product(merged, chosen[3], "sce,ed->scd")[:, :, None]


def on_device(n, stem_tensor, branch_tensors, branch_order):
    _, stems, held, bw, _ = stem_tensor.shape
    rows = bw // n
    fits = stems == held == 1 and rows % 8 == 0 and 3 * rows <= LANES and n & (n - 1) == 0 and n * rows == bw
    if fits and bw % (4 * LANES) == 0:
        return fused(n, stem_tensor, branch_tensors, branch_order)
    return plain(stem_tensor, branch_tensors, branch_order)


def solution(mesh):
    return jax.shard_map(
        functools.partial(on_device, mesh.shape["mode"]),
        mesh=mesh,
        in_specs=(P(None, "cuts", "mode", None, None), P(), P()),
        out_specs=P(None, "cuts", "mode", None, None),
        check_vma=False,
    )
```

```python
import functools

import jax
import jax.numpy as jnp
from jax import lax
from jax.experimental import pallas as pl
from jax.experimental.pallas import tpu as pltpu
from jax.sharding import PartitionSpec as P

MESH = pl.DeviceIdType.MESH
LANES = 128
F32, BF16 = jnp.float32, jnp.bfloat16


def flip(value, mask, size):
    result, bit = 0, 1
    while bit < size:
        digit = lax.rem(lax.div(value, bit), 2)
        result = result + (1 - digit if (mask // bit) % 2 else digit) * bit
        bit *= 2
    return result


def xor(a, b, size):
    result, bit = 0, 1
    while bit < size:
        result = result + lax.rem(lax.div(a, bit) + lax.div(b, bit), 2) * bit
        bit *= 2
    return result


def split(value):
    high = value.astype(BF16)
    return high, (value - high.astype(F32)).astype(BF16)


def dot(a, b):
    return jnp.dot(a, b, preferred_element_type=F32)


def dot3(high, low, right_high, right_low):
    return dot(high, right_high) + (dot(high, right_low) + dot(low, right_high))


def complex_rows(rows, right_high, right_low):
    m = rows.shape[0] // 2
    high, low = split(rows)
    by_real = dot3(high, low, right_high[0], right_low[0])
    by_imag = dot3(high, low, right_high[1], right_low[1])
    return by_real[:m] - by_imag[m:], by_imag[:m] + by_real[m:]


def kernel(n, order_ref, stem_ref, branch_ref, out_ref, lct, right_ref, stem, xh, xl, bh, bl, dh, dl, wh, wl,
           lch, lcl, lce, sent, got, order, order_sem, stem_sem, left_sem, branch_sem, send_sem, recv_sem, left_0, left_1, *branch):
    bw = stem.shape[1]
    rows = bw // n
    per = LANES // rows
    groups = n // per
    me = lax.axis_index("mode")
    z, q = lax.div(me, per), lax.rem(me, per)
    upper = lax.div(q, per // 2)
    sequence = [groups // 2] + [s for s in range(1, groups) if s != groups // 2] + [0]
    early = sequence[: groups // 2]
    lead, last = sequence[0], sequence[-2]

    def column(s):
        return pl.ds(pl.multiple_of(flip(z, s, groups) * LANES, LANES), LANES)

    barrier = pltpu.get_barrier_semaphore()
    for k in range(n - 1, 0, -1):
        pl.semaphore_signal(barrier, inc=1, device_id={"mode": flip(me, k, n)}, device_id_type=MESH)

    order_copy = pltpu.make_async_copy(order_ref, order, order_sem)
    order_copy.start()
    halves = [pl.ds(h * (bw // 2), bw // 2) for h in range(2)]
    left, left_copies, stem_copies = (left_0, left_1), [], []
    for h, half in enumerate(halves):
        left_copies.append(pltpu.make_async_copy(
            branch_ref.at[:, :, half, column(lead)], left[h], left_sem.at[h]))
        stem_copies.append([
            pltpu.make_async_copy(stem_ref.at[part, half], stem.at[part, half], stem_sem.at[part, h]) for part in range(2)])
        for copy in [left_copies[h]] + stem_copies[h]:
            copy.start()
    branch_copies = {
        s: pltpu.make_async_copy(branch_ref.at[:, :, :, column(s)], branch[s], branch_sem.at[s]) for s in sequence}
    order_copy.wait()
    o0, o1, o2, o3 = (order[k] for k in range(4))

    def left_rows(s):
        return jnp.concatenate([branch[s][o0, part].T for part in range(2)], axis=0)

    def first_rows(s):
        return complex_rows(left_rows(s), xh, xl)

    def partner(s, i):
        if s == lead:
            return i
        return xor(q, lax.rem(i + upper, per), per) if s == last else flip(q, i, per)

    def hop(s, i):
        j = partner(s, i)
        return pltpu.make_async_remote_copy(
            src_ref=sent.at[s, j], dst_ref=got.at[s, q], send_sem=send_sem.at[s, i], recv_sem=recv_sem.at[s, q],
            device_id={"mode": flip(z, s, groups) * per + j}, device_id_type=MESH)

    def own(s):
        return pltpu.make_async_copy(sent.at[s, q], got.at[s, q], recv_sem.at[s, q])

    def send(s, real, imag, which=range(per)):
        for place, j in enumerate(which):
            sent[s, j, 0] = real[place * rows:(place + 1) * rows]
            sent[s, j, 1] = imag[place * rows:(place + 1) * rows]
        for i in which:
            own(s).start() if s == 0 and i == 0 else hop(s, i).start()

    highs, lows = [], []
    part_rows = LANES // 2
    by = [None, None]
    for h, half in enumerate(halves):
        left_copies[h].wait()
        high, low = split(jnp.concatenate(
            [left[h][o0, part].T[m * part_rows:(m + 1) * part_rows] for m in range(2) for part in range(2)], axis=0))
        highs.append(high)
        lows.append(low)
        for part in range(2):
            stem_copies[h][part].wait()
            if h == part == 1:
                for s in sequence[1:] + [lead]:
                    branch_copies[s].start()
            xh[part, half], xl[part, half] = split(stem[part, half])
            add = dot3(high[:LANES], low[:LANES], xh[part, half], xl[part, half])
            by[part] = add if h == 0 else by[part] + add
    pl.semaphore_wait(barrier, n - 1)
    send(lead, by[0][:part_rows] - by[1][part_rows:], by[1][:part_rows] + by[0][part_rows:], range(per // 2))
    high, low = (jnp.concatenate([piece[LANES:] for piece in pieces], axis=1) for pieces in (highs, lows))
    by = [dot3(high, low, xh[part], xl[part]) for part in range(2)]
    send(lead, by[0][:part_rows] - by[1][part_rows:], by[1][:part_rows] + by[0][part_rows:], range(per // 2, per))
    for s in early[1:]:
        branch_copies[s].wait()
        send(s, *first_rows(s))
    for s in sequence[len(early):] + [lead]:
        branch_copies[s].wait()

    for s in range(groups):
        for part in range(2):
            bh[part, :, column(s)], bl[part, :, column(s)] = split(branch[s][o1, part])
            dh[part, :, column(s)], dl[part, :, column(s)] = split(branch[s][o3, part])

    def both(i, carry):
        at = pl.ds(pl.multiple_of(i * LANES, LANES), LANES)
        high = jnp.concatenate([bh[0, at], bh[1, at]], axis=0)
        low = jnp.concatenate([bl[0, at], bl[1, at]], axis=0)
        by_real = dot3(high, low, dh[0], dl[0])
        by_imag = dot3(high, low, dh[1], dl[1])
        wh[0, at], wl[0, at] = split(by_real[:LANES] - by_imag[LANES:])
        wh[1, at], wl[1, at] = split(by_imag[:LANES] + by_real[LANES:])
        return carry

    lax.fori_loop(0, bw // LANES, both, 0)

    for s in sequence[len(early):]:
        real, imag = first_rows(s)
        send(s, *complex_rows(jnp.concatenate([real, imag], axis=0), wh, wl))

    def third_rows(t, part, s):
        if s != last:
            return branch[t][o2, part, column(s), :]
        base = flip(z, s, groups) * LANES
        return jnp.concatenate([
            branch[t][o2, part, pl.ds(pl.multiple_of(base + partner(s, i) * rows, rows), rows), :]
            for i in range(per)], axis=0)

    pairs = ((lce, 0, LANES - 2 * rows), (lct, LANES - 2 * rows, LANES))
    for s in range(groups):
        for t in range(groups):
            real, imag = (split(third_rows(t, part, s).T) for part in range(2))
            top = column(t)
            low_half = pl.ds(pl.multiple_of(bw + flip(z, t, groups) * LANES, LANES), LANES)
            if s != last:
                for ref, r, i in ((lch, real[0], imag[0]), (lcl, real[1], imag[1])):
                    ref[s, top, :LANES] = r
                    ref[s, top, LANES:] = -i
                    ref[s, low_half, :LANES] = i
                    ref[s, low_half, LANES:] = r
                continue
            for ref, begin, end in pairs:
                for place, (r, i) in enumerate(((real[0], imag[0]), (real[0], imag[0]), (real[1], imag[1]))):
                    at = slice(2 * place * (end - begin), (2 * place + 1) * (end - begin))
                    after = slice((2 * place + 1) * (end - begin), (2 * place + 2) * (end - begin))
                    ref[top, at] = r[:, begin:end]
                    ref[top, after] = -i[:, begin:end]
                    ref[low_half, at] = i[:, begin:end]
                    ref[low_half, after] = r[:, begin:end]

    arrivals = [0] + [s for s in early if s != groups // 2] + [groups // 2] + [s for s in sequence[len(early):] if s]
    tile = 2 * LANES

    def arrive(s, j):
        pltpu.make_async_copy(got.at[s, j], got.at[s, j], recv_sem.at[s, j]).wait()

    def result(i):
        part, row = divmod(i * tile, bw)
        return part, slice(row, row + tile)

    def stacked(places):
        for i in places:
            arrive(last, partner(last, i))
        high, low = split(jnp.concatenate([got[last, partner(last, i), part] for part in range(2) for i in places], axis=0))
        return jnp.concatenate([high, low, high], axis=0)

    for index, s in enumerate(arrivals):
        if s == last:
            right = stacked(range(per - 2))
        else:
            for j in range(per):
                arrive(s, j)
            arrived = jnp.concatenate([got[s, j, part] for part in range(2) for j in range(per)], axis=0)
            if s in early:
                arrived = jnp.concatenate(complex_rows(arrived, wh, wl), axis=0)
            right_high, right_low = split(arrived)
        for i in range(2 * bw // tile):
            at = slice(i * tile, (i + 1) * tile)
            add = dot(lce[at], right) if s == last else dot3(lch[s, at], lcl[s, at], right_high, right_low)
            out_ref[result(i)] = add if index == 0 else out_ref[result(i)] + add
    for s in range(groups):
        for i in range(per):
            if s or i:
                hop(s, i).wait_send()
    right_ref[...] = stacked(range(per - 2, per))


def finish(acc_ref, left_ref, right_ref, out_ref, tiles, sem):
    count, tile, bw = tiles.shape
    right = right_ref[...]
    copies = []
    for i in range(count):
        part, row = divmod(i * tile, bw)
        at = slice(i * tile, (i + 1) * tile)
        tiles[i] = acc_ref[part, row:row + tile] + dot(left_ref[at], right)
        copies.append(pltpu.make_async_copy(tiles.at[i], out_ref.at[part, pl.ds(row, tile)], sem.at[i]))
        copies[i].start()
    for copy in copies:
        copy.wait()


def fused(n, stem_tensor, branch_tensors, branch_order):
    bw = stem_tensor.shape[-1]
    rows = bw // n
    per = LANES // rows
    groups = n // per
    square = pltpu.VMEM((2, bw, bw), BF16)
    hbm = functools.partial(pltpu.with_memory_space_constraint, memory_space=pltpu.HBM)
    window = pltpu.VMEM((groups, 2 * bw, 2 * LANES), BF16)
    vmem = pl.BlockSpec(memory_space=pltpu.VMEM)
    tiles = 2 * bw // LANES
    partial = pl.pallas_call(
        functools.partial(kernel, n),
        out_shape=[
            jax.ShapeDtypeStruct((2, bw, bw), F32),
            jax.ShapeDtypeStruct((2 * bw, 12 * rows), BF16),
            jax.ShapeDtypeStruct((12 * rows, bw), BF16),
        ],
        in_specs=[pl.BlockSpec(memory_space=pl.ANY)] * 3,
        out_specs=[vmem] * 3,
        scratch_shapes=[
            pltpu.VMEM((2, bw, bw), F32),
            *[square] * 8,
            window,
            window,
            pltpu.VMEM((2 * bw, 6 * (LANES - 2 * rows)), BF16),
            pltpu.VMEM((groups, per, 2, rows, bw), F32),
            pltpu.VMEM((groups, per, 2, rows, bw), F32),
            pltpu.SMEM(branch_order.shape, jnp.int32),
            pltpu.SemaphoreType.DMA,
            pltpu.SemaphoreType.DMA((2, 2)),
            pltpu.SemaphoreType.DMA((2,)),
            pltpu.SemaphoreType.DMA((groups,)),
            pltpu.SemaphoreType.DMA((groups, per)),
            pltpu.SemaphoreType.DMA((groups, per)),
            *[pltpu.VMEM((4, 2, bw // 2, LANES), F32)] * 2,
            *[pltpu.VMEM((4, 2, bw, LANES), F32)] * groups,
        ],
        compiler_params=pltpu.CompilerParams(collective_id=0, has_side_effects=True, vmem_limit_bytes=40 << 20),
    )(hbm(branch_order), hbm(stem_tensor.reshape(2, bw, bw)), hbm(branch_tensors))
    return pl.pallas_call(
        finish,
        out_shape=jax.ShapeDtypeStruct((2, bw, bw), F32),
        in_specs=[vmem] * 3,
        out_specs=pl.BlockSpec(memory_space=pl.ANY),
        scratch_shapes=[pltpu.VMEM((tiles, LANES, bw), F32), pltpu.SemaphoreType.DMA((tiles,))],
        compiler_params=pltpu.CompilerParams(vmem_limit_bytes=8 << 20),
    )(*partial).reshape(stem_tensor.shape)


def complex_product(first, second, form):
    high = lax.Precision.HIGHEST
    real = jnp.einsum(form, first[0], second[0], precision=high) - jnp.einsum(form, first[1], second[1], precision=high)
    imag = jnp.einsum(form, first[0], second[1], precision=high) + jnp.einsum(form, first[1], second[0], precision=high)
    return jnp.stack([real, imag])


def plain(stem_tensor, branch_tensors, branch_order):
    field = stem_tensor[:, :, 0]
    chosen = [branch_tensors[branch_order[index]] for index in range(4)]
    field = complex_product(field, chosen[0], "sce,cd->sde")
    field = complex_product(field, chosen[1], "sce,ed->scd")
    moved = lax.all_to_all(field[:, :, None], "mode", split_axis=3, concat_axis=2, tiled=True)
    merged = moved.reshape(field.shape)
    merged = complex_product(merged, chosen[2], "sce,cd->sde")
    return complex_product(merged, chosen[3], "sce,ed->scd")[:, :, None]


def on_device(n, stem_tensor, branch_tensors, branch_order):
    _, stems, held, bw, _ = stem_tensor.shape
    rows = bw // n
    fits = stems == held == 1 and rows % 8 == 0 and 3 * rows <= LANES and n & (n - 1) == 0 and n * rows == bw
    if fits and bw % (4 * LANES) == 0:
        return fused(n, stem_tensor, branch_tensors, branch_order)
    return plain(stem_tensor, branch_tensors, branch_order)


def solution(mesh):
    return jax.shard_map(
        functools.partial(on_device, mesh.shape["mode"]),
        mesh=mesh,
        in_specs=(P(None, "cuts", "mode", None, None), P(), P()),
        out_specs=P(None, "cuts", "mode", None, None),
        check_vma=False,
    )
```

```python
import functools

import jax
import jax.numpy as jnp
from jax import lax
from jax.experimental import pallas as pl
from jax.experimental.pallas import tpu as pltpu
from jax.sharding import PartitionSpec as P

MESH = pl.DeviceIdType.MESH
LANES = 128
HEAD = 1
F32, BF16 = jnp.float32, jnp.bfloat16


def flip(value, mask, size):
    result, bit = 0, 1
    while bit < size:
        digit = lax.rem(lax.div(value, bit), 2)
        result = result + (1 - digit if (mask // bit) % 2 else digit) * bit
        bit *= 2
    return result


def split(value):
    high = value.astype(BF16)
    return high, (value - high.astype(F32)).astype(BF16)


def dot(a, b):
    return jnp.dot(a, b, preferred_element_type=F32)


def dot3(high, low, right_high, right_low):
    return dot(high, right_high) + (dot(high, right_low) + dot(low, right_high))


def complex_rows(rows, right_high, right_low):
    m = rows.shape[0] // 2
    high, low = split(rows)
    by_real = dot3(high, low, right_high[0], right_low[0])
    by_imag = dot3(high, low, right_high[1], right_low[1])
    return by_real[:m] - by_imag[m:], by_imag[:m] + by_real[m:]


def kernel(n, order_ref, stem_ref, branch_ref, out_ref, last_high, last_low, tail_high, tail_low, stem, xh, xl, bh, bl, dh, dl, wh, wl,
           lch, lcl, sent, got, order, order_sem, stem_sem, left_sem, branch_sem, send_sem, recv_sem, last_sem, left_0, left_1, *branch):
    bw = stem.shape[1]
    rows = bw // n
    per = LANES // rows
    groups = n // per
    me = lax.axis_index("mode")
    z, q = lax.div(me, per), lax.rem(me, per)
    upper = lax.div(q, per // 2)
    sequence = [groups // 2] + [s for s in range(1, groups) if s != groups // 2] + [0]
    early = sequence[: groups // 2]
    lead, last = sequence[0], sequence[-2]

    def column(s):
        return pl.ds(pl.multiple_of(flip(z, s, groups) * LANES, LANES), LANES)

    barrier = pltpu.get_barrier_semaphore()
    for k in range(n - 1, 0, -1):
        pl.semaphore_signal(barrier, inc=1, device_id={"mode": flip(me, k, n)}, device_id_type=MESH)

    order_copy = pltpu.make_async_copy(order_ref, order, order_sem)
    order_copy.start()
    halves = [pl.ds(h * (bw // 2), bw // 2) for h in range(2)]
    left = (left_0, left_1)
    left_copies = [pltpu.make_async_copy(
        branch_ref.at[:, :, half, column(lead)], left[h], left_sem.at[h]) for h, half in enumerate(halves)]
    stem_copies = [[pltpu.make_async_copy(
        stem_ref.at[part, half], stem.at[part, half], stem_sem.at[part, h]) for part in range(2)] for h, half in enumerate(halves)]
    for copy in (left_copies[0], *stem_copies[0], left_copies[1], *stem_copies[1]):
        copy.start()
    branch_copies = {
        s: pltpu.make_async_copy(branch_ref.at[:, :, :, column(s)], branch[s], branch_sem.at[s]) for s in sequence}
    order_copy.wait()
    o0, o1, o2, o3 = (order[k] for k in range(4))

    def left_rows(s):
        return jnp.concatenate([branch[s][o0, part].T for part in range(2)], axis=0)

    def first_rows(s):
        return complex_rows(left_rows(s), xh, xl)

    def partner(s, i):
        if s == lead:
            return i
        if s != last:
            return flip(q, i, per)
        column = upper if i >= per // 2 else 1 - upper
        return column * (per // 2) + (per - 1 - i) % (per // 2)

    def hop(s, i, h=None):
        j = partner(s, i)
        where = () if h is None else (slice(None), slice(None), halves[h])
        return pltpu.make_async_remote_copy(
            src_ref=sent.at[(s, j, *where)], dst_ref=got.at[(s, q, *where)], send_sem=send_sem.at[s],
            recv_sem=recv_sem.at[s] if h is None else last_sem.at[h],
            device_id={"mode": flip(z, s, groups) * per + j}, device_id_type=MESH)

    def own(s):
        return pltpu.make_async_copy(sent.at[s, q], got.at[s, q], recv_sem.at[s])

    def send(s, real, imag, which=range(per)):
        for place, j in enumerate(which):
            sent[s, j, 0] = real[place * rows:(place + 1) * rows]
            sent[s, j, 1] = imag[place * rows:(place + 1) * rows]
        for h in range(2) if s == last else [None]:
            for i in which:
                own(s).start() if s == 0 and i == 0 else hop(s, i, h).start()

    highs, lows = [], []
    parcels = [range(HEAD), range(HEAD, per)]
    cut = 2 * HEAD * rows
    by = [None, None]

    def send_lead(by, which):
        m = by[0].shape[0] // 2
        send(lead, by[0][:m] - by[1][m:], by[1][:m] + by[0][m:], which)

    for h, half in enumerate(halves):
        left_copies[h].wait()
        high, low = split(jnp.concatenate([
            left[h][o0, part].T[which[0] * rows:(which[-1] + 1) * rows] for which in parcels for part in range(2)], axis=0))
        highs.append(high)
        lows.append(low)
        for part in range(2):
            stem_copies[h][part].wait()
            if h == part == 1:
                for s in sequence[1:] + [lead]:
                    branch_copies[s].start()
            xh[part, half], xl[part, half] = split(stem[part, half])
            both_parts = dot(jnp.concatenate([high[:cut], low[:cut]], axis=0), xh[part, half])
            add = both_parts[:cut] + (both_parts[cut:] + dot(high[:cut], xl[part, half]))
            by[part] = add if h == 0 else by[part] + add
    pl.semaphore_wait(barrier, n - 1)
    send_lead(by, parcels[0])
    high, low = (jnp.concatenate([piece[cut:] for piece in pieces], axis=1) for pieces in (highs, lows))
    send_lead([dot3(high, low, xh[part], xl[part]) for part in range(2)], parcels[1])
    for s in early[1:]:
        branch_copies[s].wait()
        send(s, *first_rows(s))
    for s in sequence[len(early):] + [lead]:
        branch_copies[s].wait()

    for s in range(groups):
        for part in range(2):
            bh[part, :, column(s)], bl[part, :, column(s)] = split(branch[s][o1, part])
            dh[part, :, column(s)], dl[part, :, column(s)] = split(branch[s][o3, part])

    def both(i, carry):
        at = pl.ds(pl.multiple_of(i * LANES, LANES), LANES)
        high = jnp.concatenate([bh[0, at], bh[1, at]], axis=0)
        low = jnp.concatenate([bl[0, at], bl[1, at]], axis=0)
        by_real = dot3(high, low, dh[0], dl[0])
        by_imag = dot3(high, low, dh[1], dl[1])
        wh[0, at], wl[0, at] = split(by_real[:LANES] - by_imag[LANES:])
        wh[1, at], wl[1, at] = split(by_imag[:LANES] + by_real[LANES:])
        return carry

    lax.fori_loop(0, bw // LANES, both, 0)

    for s in sequence[len(early):]:
        real, imag = first_rows(s)
        send(s, *complex_rows(jnp.concatenate([real, imag], axis=0), wh, wl))

    for s in range(groups):
        high_ref, low_ref = (last_high, last_low) if s == last else (lch.at[s], lcl.at[s])
        for t in range(groups):
            real, imag = (split(branch[t][o2, part, column(s), :].T) for part in range(2))
            top = column(t)
            low_half = pl.ds(pl.multiple_of(bw + flip(z, t, groups) * LANES, LANES), LANES)
            for ref, r, i in ((high_ref, real[0], imag[0]), (low_ref, real[1], imag[1])):
                ref[top, :LANES] = r
                ref[top, LANES:] = -i
                ref[low_half, :LANES] = i
                ref[low_half, LANES:] = r

    arrivals = [0] + [s for s in early if s != groups // 2] + [groups // 2] + [s for s in sequence[len(early):] if s]
    tile = 2 * LANES

    def await_bytes(place, sem):
        pltpu.make_async_copy(place, place, sem).wait()

    def arrived(s, side):
        return jnp.concatenate([got[s, j, part, :, side] for part in range(2) for j in range(per)], axis=0)

    for index, s in enumerate(arrivals):
        if s == last:
            await_bytes(got.at[last, :, :, :, halves[0]], last_sem.at[0])
            side = slice(0, bw // 2)
        else:
            await_bytes(got.at[s], recv_sem.at[s])
            side = slice(0, bw)
        right = arrived(s, side)
        if s in early:
            right = jnp.concatenate(complex_rows(right, wh, wl), axis=0)
        right_high, right_low = split(right)
        high_ref, low_ref = (last_high, last_low) if s == last else (lch.at[s], lcl.at[s])
        for i in range(2 * bw // tile):
            at = slice(i * tile, (i + 1) * tile)
            part, row = divmod(i * tile, bw)
            place = (part, slice(row, row + tile), side)
            add = dot3(high_ref[at], low_ref[at], right_high, right_low)
            out_ref[place] = add if index == 0 else out_ref[place] + add
    for s in range(groups):
        await_bytes(sent.at[s, pl.ds(0, per if s else per - 1)], send_sem.at[s])
    await_bytes(got.at[last, :, :, :, halves[1]], last_sem.at[1])
    tail_high[...], tail_low[...] = split(arrived(last, slice(bw // 2, bw)))


def finish(acc_ref, high_ref, low_ref, right_high, right_low, out_ref, tiles, side_sem, sem):
    count, tile, half = tiles.shape
    copies = []
    for part in range(2):
        at = (part, slice(None), pl.ds(0, half))
        copies.append(pltpu.make_async_copy(acc_ref.at[at], out_ref.at[at], side_sem.at[part]))
        copies[part].start()
    right = right_high[...], right_low[...]
    for i in range(count):
        part, row = divmod(i * tile, 2 * half)
        at = slice(i * tile, (i + 1) * tile)
        tiles[i] = acc_ref[part, row:row + tile, half:] + dot3(high_ref[at], low_ref[at], *right)
        copies.append(pltpu.make_async_copy(tiles.at[i], out_ref.at[part, pl.ds(row, tile), pl.ds(half, half)], sem.at[i]))
        copies[-1].start()
    for copy in copies:
        copy.wait()


def fused(n, stem_tensor, branch_tensors, branch_order):
    bw = stem_tensor.shape[-1]
    rows = bw // n
    per = LANES // rows
    groups = n // per
    square = pltpu.VMEM((2, bw, bw), BF16)
    hbm = functools.partial(pltpu.with_memory_space_constraint, memory_space=pltpu.HBM)
    window = pltpu.VMEM((groups, 2 * bw, 2 * LANES), BF16)
    vmem = pl.BlockSpec(memory_space=pltpu.VMEM)
    tiles = 2 * bw // LANES
    partial = pl.pallas_call(
        functools.partial(kernel, n),
        out_shape=[
            jax.ShapeDtypeStruct((2, bw, bw), F32),
            *[jax.ShapeDtypeStruct((2 * bw, 2 * LANES), BF16)] * 2,
            *[jax.ShapeDtypeStruct((2 * LANES, bw // 2), BF16)] * 2,
        ],
        in_specs=[pl.BlockSpec(memory_space=pl.ANY)] * 3,
        out_specs=[vmem] * 5,
        scratch_shapes=[
            pltpu.VMEM((2, bw, bw), F32),
            *[square] * 8,
            window,
            window,
            pltpu.VMEM((groups, per, 2, rows, bw), F32),
            pltpu.VMEM((groups, per, 2, rows, bw), F32),
            pltpu.SMEM(branch_order.shape, jnp.int32),
            pltpu.SemaphoreType.DMA,
            pltpu.SemaphoreType.DMA((2, 2)),
            pltpu.SemaphoreType.DMA((2,)),
            pltpu.SemaphoreType.DMA((groups,)),
            pltpu.SemaphoreType.DMA((groups,)),
            pltpu.SemaphoreType.DMA((groups,)),
            pltpu.SemaphoreType.DMA((2,)),
            *[pltpu.VMEM((4, 2, bw // 2, LANES), F32)] * 2,
            *[pltpu.VMEM((4, 2, bw, LANES), F32)] * groups,
        ],
        compiler_params=pltpu.CompilerParams(collective_id=0, has_side_effects=True, vmem_limit_bytes=40 << 20),
    )(hbm(branch_order), hbm(stem_tensor.reshape(2, bw, bw)), hbm(branch_tensors))
    return pl.pallas_call(
        finish,
        out_shape=jax.ShapeDtypeStruct((2, bw, bw), F32),
        in_specs=[vmem] * 5,
        out_specs=pl.BlockSpec(memory_space=pl.ANY),
        scratch_shapes=[pltpu.VMEM((tiles, LANES, bw // 2), F32), pltpu.SemaphoreType.DMA((2,)), pltpu.SemaphoreType.DMA((tiles,))],
        compiler_params=pltpu.CompilerParams(vmem_limit_bytes=8 << 20),
    )(*partial).reshape(stem_tensor.shape)


def complex_product(first, second, form):
    high = lax.Precision.HIGHEST
    real = jnp.einsum(form, first[0], second[0], precision=high) - jnp.einsum(form, first[1], second[1], precision=high)
    imag = jnp.einsum(form, first[0], second[1], precision=high) + jnp.einsum(form, first[1], second[0], precision=high)
    return jnp.stack([real, imag])


def plain(stem_tensor, branch_tensors, branch_order):
    field = stem_tensor[:, :, 0]
    chosen = [branch_tensors[branch_order[index]] for index in range(4)]
    field = complex_product(field, chosen[0], "sce,cd->sde")
    field = complex_product(field, chosen[1], "sce,ed->scd")
    moved = lax.all_to_all(field[:, :, None], "mode", split_axis=3, concat_axis=2, tiled=True)
    merged = moved.reshape(field.shape)
    merged = complex_product(merged, chosen[2], "sce,cd->sde")
    return complex_product(merged, chosen[3], "sce,ed->scd")[:, :, None]


def on_device(n, stem_tensor, branch_tensors, branch_order):
    _, stems, held, bw, _ = stem_tensor.shape
    rows = bw // n
    fits = stems == held == 1 and rows % 8 == 0 and 3 * rows <= LANES and n & (n - 1) == 0 and n * rows == bw
    if fits and bw % (4 * LANES) == 0:
        return fused(n, stem_tensor, branch_tensors, branch_order)
    return plain(stem_tensor, branch_tensors, branch_order)


def solution(mesh):
    return jax.shard_map(
        functools.partial(on_device, mesh.shape["mode"]),
        mesh=mesh,
        in_specs=(P(None, "cuts", "mode", None, None), P(), P()),
        out_specs=P(None, "cuts", "mode", None, None),
        check_vma=False,
    )
```

```python
import functools

import jax
import jax.numpy as jnp
from jax import lax
from jax.experimental import pallas as pl
from jax.experimental.pallas import tpu as pltpu
from jax.sharding import PartitionSpec as P

MESH = pl.DeviceIdType.MESH
LANES = 128
F32, BF16 = jnp.float32, jnp.bfloat16


def flip(value, mask, size):
    result, bit = 0, 1
    while bit < size:
        digit = lax.rem(lax.div(value, bit), 2)
        result = result + (1 - digit if (mask // bit) % 2 else digit) * bit
        bit *= 2
    return result


def split(value):
    high = value.astype(BF16)
    return high, (value - high.astype(F32)).astype(BF16)


def dot(a, b):
    return jnp.dot(a, b, preferred_element_type=F32)


def dot3(high, low, right_high, right_low):
    return dot(high, right_high) + (dot(high, right_low) + dot(low, right_high))


def complex_rows(rows, right_high, right_low):
    m = rows.shape[0] // 2
    high, low = split(rows)
    by_real = dot3(high, low, right_high[0], right_low[0])
    by_imag = dot3(high, low, right_high[1], right_low[1])
    return by_real[:m] - by_imag[m:], by_imag[:m] + by_real[m:]


def kernel(n, order_ref, stem_ref, branch_ref, out_ref, last_high, last_low, tail_high, tail_low, stem, xh, xl, bh, bl, dh, dl, wh, wl,
           lch, lcl, sent, got, order, order_sem, stem_sem, left_sem, branch_sem, send_sem, recv_sem, last_sem, side_sem, notice_low, notice_top, left_0, left_1, *branch):
    bw = stem.shape[1]
    rows = bw // n
    per = LANES // rows
    groups = n // per
    me = lax.axis_index("mode")
    z, q = lax.div(me, per), lax.rem(me, per)
    upper = lax.div(q, per // 2)
    sequence = [groups // 2] + [s for s in range(1, groups) if s != groups // 2] + [0]
    early = sequence[: groups // 2]
    lead, last = sequence[0], sequence[-2]

    def column(s):
        return pl.ds(pl.multiple_of(flip(z, s, groups) * LANES, LANES), LANES)

    barrier = pltpu.get_barrier_semaphore()
    top, middle = groups - 1, groups // 2
    near = middle ^ top

    def greet(sem, s, k):
        pl.semaphore_signal(
            sem, inc=1, device_id={"mode": flip(z, s, groups) * per + flip(q, k, per)}, device_id_type=MESH)

    for s in range(groups - 1, -1, -1):
        for k in range(per):
            if s == near:
                pl.when(z != top)(functools.partial(greet, barrier, s, k))
            elif s == lead:
                pl.when(z + upper != top + 1)(functools.partial(greet, barrier, s, k))
            elif s or k:
                greet(barrier, s, k)

    def equal(a, b):
        return (a == b).astype(jnp.int32)

    def enter():
        pl.semaphore_wait(barrier, n - 1 - per * equal(z, middle) - per // 2 * equal(z, middle - 1))
        for k in range(per):
            pl.when(z == top)(functools.partial(greet, notice_low, near, k))
            pl.when(z + upper == top + 1)(functools.partial(greet, notice_top, lead, k))

    order_copy = pltpu.make_async_copy(order_ref, order, order_sem)
    order_copy.start()
    halves = [pl.ds(h * (bw // 2), bw // 2) for h in range(2)]
    left = (left_0, left_1)
    left_copies = [pltpu.make_async_copy(
        branch_ref.at[:, :, half, column(lead)], left[h], left_sem.at[h]) for h, half in enumerate(halves)]
    stem_copies = [pltpu.make_async_copy(
        stem_ref.at[:, half, halves[0]], stem.at[:, half, halves[0]], stem_sem.at[k]) for k, half in enumerate(halves)]
    side_copy = pltpu.make_async_copy(stem_ref.at[:, :, halves[1]], stem.at[:, :, halves[1]], side_sem)
    for copy in (left_copies[0], stem_copies[0], left_copies[1], stem_copies[1], side_copy):
        copy.start()
    branch_copies = {
        s: pltpu.make_async_copy(branch_ref.at[:, :, :, column(s)], branch[s], branch_sem.at[s]) for s in sequence}
    order_copy.wait()
    o0, o1, o2, o3 = (order[k] for k in range(4))

    def left_rows(s):
        return jnp.concatenate([branch[s][o0, part].T for part in range(2)], axis=0)

    def first_rows(s):
        return complex_rows(left_rows(s), xh, xl)

    def partner(s, i):
        if s == lead:
            return i
        if s != last:
            return flip(q, i, per)
        column = upper if i >= per // 2 else 1 - upper
        return column * (per // 2) + (per - 1 - i) % (per // 2)

    def hop(s, i, h=None):
        j = partner(s, i)
        where = () if h is None else (slice(None), slice(None), halves[h])
        return pltpu.make_async_remote_copy(
            src_ref=sent.at[(s, j, *where)], dst_ref=got.at[(s, q, *where)], send_sem=send_sem.at[s],
            recv_sem=last_sem.at[h] if s == last else recv_sem.at[s],
            device_id={"mode": flip(z, s, groups) * per + j}, device_id_type=MESH)

    def await_bytes(place, sem):
        pltpu.make_async_copy(place, place, sem).wait()

    def own(s):
        return pltpu.make_async_copy(sent.at[s, q], got.at[s, q], recv_sem.at[s])

    def send(s, real, imag, which=range(per)):
        for place, j in enumerate(which):
            sent[s, j, 0] = real[place * rows:(place + 1) * rows]
            sent[s, j, 1] = imag[place * rows:(place + 1) * rows]
        for h in range(2) if s == last else [None]:
            for i in which:
                own(s).start() if s == 0 and i == 0 else hop(s, i, h).start()

    highs, lows = [], []
    parcels = [range(per // 2), range(per // 2, per)]
    by = [None, None]

    def send_lead(by, which, h=None):
        m = by[0].shape[0] // 2
        side = slice(None) if h is None else slice(h * (bw // 2), (h + 1) * (bw // 2))
        for part, value in enumerate((by[0][:m] - by[1][m:], by[1][:m] + by[0][m:])):
            for place, j in enumerate(which):
                sent[lead, j, part, :, side] = value[place * rows:(place + 1) * rows]
        for j in which:
            hop(lead, j, h).start()

    left_side, right_side = slice(0, bw // 2), slice(bw // 2, bw)
    for k, half in enumerate(halves):
        left_copies[k].wait()
        high, low = split(jnp.concatenate([
            left[k][o0, part].T[which[0] * rows:(which[-1] + 1) * rows] for which in parcels for part in range(2)], axis=0))
        highs.append(high)
        lows.append(low)
        stem_copies[k].wait()
        for part in range(2):
            xh[part, half, left_side], xl[part, half, left_side] = split(stem[part, half, left_side])
            add = dot3(high[:LANES], low[:LANES], xh[part, half, left_side], xl[part, half, left_side])
            by[part] = add if k == 0 else by[part] + add
    enter()
    send_lead(by, parcels[0], 0)
    side_copy.wait()
    for s in sequence[1:] + [lead]:
        branch_copies[s].start()
    for part in range(2):
        xh[part, :, right_side], xl[part, :, right_side] = split(stem[part, :, right_side])
    high, low = (jnp.concatenate([piece[:LANES] for piece in pieces], axis=1) for pieces in (highs, lows))
    send_lead([dot3(high, low, xh[part, :, right_side], xl[part, :, right_side]) for part in range(2)], parcels[0], 1)
    high, low = (jnp.concatenate([piece[LANES:] for piece in pieces], axis=1) for pieces in (highs, lows))
    rest = [dot3(high, low, xh[part], xl[part]) for part in range(2)]
    pl.when(z == middle - 1)(lambda: pl.semaphore_wait(notice_top, per // 2))
    send_lead(rest, parcels[1])
    for s in early[1:]:
        branch_copies[s].wait()
        if s == near:
            pl.when(z == middle)(lambda: pl.semaphore_wait(notice_low, per))
        send(s, *first_rows(s))
    for s in sequence[len(early):] + [lead]:
        branch_copies[s].wait()

    for s in range(groups):
        for part in range(2):
            bh[part, :, column(s)], bl[part, :, column(s)] = split(branch[s][o1, part])
            dh[part, :, column(s)], dl[part, :, column(s)] = split(branch[s][o3, part])

    def both(i, carry):
        at = pl.ds(pl.multiple_of(i * LANES, LANES), LANES)
        high = jnp.concatenate([bh[0, at], bh[1, at]], axis=0)
        low = jnp.concatenate([bl[0, at], bl[1, at]], axis=0)
        by_real = dot3(high, low, dh[0], dl[0])
        by_imag = dot3(high, low, dh[1], dl[1])
        wh[0, at], wl[0, at] = split(by_real[:LANES] - by_imag[LANES:])
        wh[1, at], wl[1, at] = split(by_imag[:LANES] + by_real[LANES:])
        return carry

    lax.fori_loop(0, bw // LANES, both, 0)

    for s in sequence[len(early):]:
        real, imag = first_rows(s)
        send(s, *complex_rows(jnp.concatenate([real, imag], axis=0), wh, wl))

    for s in range(groups):
        high_ref, low_ref = (last_high, last_low) if s == last else (lch.at[s], lcl.at[s])
        for t in range(groups):
            real, imag = (split(branch[t][o2, part, column(s), :].T) for part in range(2))
            top = column(t)
            low_half = pl.ds(pl.multiple_of(bw + flip(z, t, groups) * LANES, LANES), LANES)
            for ref, r, i in ((high_ref, real[0], imag[0]), (low_ref, real[1], imag[1])):
                ref[top, :LANES] = r
                ref[top, LANES:] = -i
                ref[low_half, :LANES] = i
                ref[low_half, LANES:] = r

    arrivals = [0] + [s for s in early if s != groups // 2] + [groups // 2] + [s for s in sequence[len(early):] if s]
    tile = 2 * LANES

    def arrived(s, side):
        return jnp.concatenate([got[s, j, part, :, side] for part in range(2) for j in range(per)], axis=0)

    for index, s in enumerate(arrivals):
        if s == last:
            await_bytes(got.at[last, :, :, :, halves[0]], last_sem.at[0])
            side = slice(0, bw // 2)
        else:
            await_bytes(got.at[s], recv_sem.at[s])
            side = slice(0, bw)
        right = arrived(s, side)
        if s in early:
            right = jnp.concatenate(complex_rows(right, wh, wl), axis=0)
        right_high, right_low = split(right)
        high_ref, low_ref = (last_high, last_low) if s == last else (lch.at[s], lcl.at[s])
        for i in range(2 * bw // tile):
            at = slice(i * tile, (i + 1) * tile)
            part, row = divmod(i * tile, bw)
            place = (part, slice(row, row + tile), side)
            add = dot3(high_ref[at], low_ref[at], right_high, right_low)
            out_ref[place] = add if index == 0 else out_ref[place] + add
    for s in range(groups):
        await_bytes(sent.at[s, pl.ds(0, per if s else per - 1)], send_sem.at[s])
    await_bytes(got.at[last, :, :, :, halves[1]], last_sem.at[1])
    tail_high[...], tail_low[...] = split(arrived(last, slice(bw // 2, bw)))


def finish(acc_ref, high_ref, low_ref, right_high, right_low, out_ref, tiles, side_sem, sem):
    count, tile, half = tiles.shape
    copies = []
    for part in range(2):
        at = (part, slice(None), pl.ds(0, half))
        copies.append(pltpu.make_async_copy(acc_ref.at[at], out_ref.at[at], side_sem.at[part]))
        copies[part].start()
    right = right_high[...], right_low[...]
    for i in range(count):
        part, row = divmod(i * tile, 2 * half)
        at = slice(i * tile, (i + 1) * tile)
        tiles[i] = acc_ref[part, row:row + tile, half:] + dot3(high_ref[at], low_ref[at], *right)
        copies.append(pltpu.make_async_copy(tiles.at[i], out_ref.at[part, pl.ds(row, tile), pl.ds(half, half)], sem.at[i]))
        copies[-1].start()
    for copy in copies:
        copy.wait()


def fused(n, stem_tensor, branch_tensors, branch_order):
    bw = stem_tensor.shape[-1]
    rows = bw // n
    per = LANES // rows
    groups = n // per
    square = pltpu.VMEM((2, bw, bw), BF16)
    hbm = functools.partial(pltpu.with_memory_space_constraint, memory_space=pltpu.HBM)
    window = pltpu.VMEM((groups, 2 * bw, 2 * LANES), BF16)
    vmem = pl.BlockSpec(memory_space=pltpu.VMEM)
    tiles = 2 * bw // LANES
    partial = pl.pallas_call(
        functools.partial(kernel, n),
        out_shape=[
            jax.ShapeDtypeStruct((2, bw, bw), F32),
            *[jax.ShapeDtypeStruct((2 * bw, 2 * LANES), BF16)] * 2,
            *[jax.ShapeDtypeStruct((2 * LANES, bw // 2), BF16)] * 2,
        ],
        in_specs=[pl.BlockSpec(memory_space=pl.ANY)] * 3,
        out_specs=[vmem] * 5,
        scratch_shapes=[
            pltpu.VMEM((2, bw, bw), F32),
            *[square] * 8,
            window,
            window,
            pltpu.VMEM((groups, per, 2, rows, bw), F32),
            pltpu.VMEM((groups, per, 2, rows, bw), F32),
            pltpu.SMEM(branch_order.shape, jnp.int32),
            pltpu.SemaphoreType.DMA,
            pltpu.SemaphoreType.DMA((2,)),
            pltpu.SemaphoreType.DMA((2,)),
            pltpu.SemaphoreType.DMA((groups,)),
            pltpu.SemaphoreType.DMA((groups,)),
            pltpu.SemaphoreType.DMA((groups,)),
            pltpu.SemaphoreType.DMA((2,)),
            pltpu.SemaphoreType.DMA,
            pltpu.SemaphoreType.REGULAR,
            pltpu.SemaphoreType.REGULAR,
            *[pltpu.VMEM((4, 2, bw // 2, LANES), F32)] * 2,
            *[pltpu.VMEM((4, 2, bw, LANES), F32)] * groups,
        ],
        compiler_params=pltpu.CompilerParams(collective_id=0, has_side_effects=True, vmem_limit_bytes=40 << 20),
    )(hbm(branch_order), hbm(stem_tensor.reshape(2, bw, bw)), hbm(branch_tensors))
    return pl.pallas_call(
        finish,
        out_shape=jax.ShapeDtypeStruct((2, bw, bw), F32),
        in_specs=[vmem] * 5,
        out_specs=pl.BlockSpec(memory_space=pl.ANY),
        scratch_shapes=[pltpu.VMEM((tiles, LANES, bw // 2), F32), pltpu.SemaphoreType.DMA((2,)), pltpu.SemaphoreType.DMA((tiles,))],
        compiler_params=pltpu.CompilerParams(vmem_limit_bytes=8 << 20),
    )(*partial).reshape(stem_tensor.shape)


def complex_product(first, second, form):
    high = lax.Precision.HIGHEST
    real = jnp.einsum(form, first[0], second[0], precision=high) - jnp.einsum(form, first[1], second[1], precision=high)
    imag = jnp.einsum(form, first[0], second[1], precision=high) + jnp.einsum(form, first[1], second[0], precision=high)
    return jnp.stack([real, imag])


def plain(stem_tensor, branch_tensors, branch_order):
    field = stem_tensor[:, :, 0]
    chosen = [branch_tensors[branch_order[index]] for index in range(4)]
    field = complex_product(field, chosen[0], "sce,cd->sde")
    field = complex_product(field, chosen[1], "sce,ed->scd")
    moved = lax.all_to_all(field[:, :, None], "mode", split_axis=3, concat_axis=2, tiled=True)
    merged = moved.reshape(field.shape)
    merged = complex_product(merged, chosen[2], "sce,cd->sde")
    return complex_product(merged, chosen[3], "sce,ed->scd")[:, :, None]


def on_device(n, stem_tensor, branch_tensors, branch_order):
    _, stems, held, bw, _ = stem_tensor.shape
    rows = bw // n
    fits = stems == held == 1 and rows % 8 == 0 and 3 * rows <= LANES and n & (n - 1) == 0 and n * rows == bw
    if fits and bw % (4 * LANES) == 0:
        return fused(n, stem_tensor, branch_tensors, branch_order)
    return plain(stem_tensor, branch_tensors, branch_order)


def solution(mesh):
    return jax.shard_map(
        functools.partial(on_device, mesh.shape["mode"]),
        mesh=mesh,
        in_specs=(P(None, "cuts", "mode", None, None), P(), P()),
        out_specs=P(None, "cuts", "mode", None, None),
        check_vma=False,
    )
```

```python
import functools

import jax
import jax.numpy as jnp
from jax import lax
from jax.experimental import pallas as pl
from jax.experimental.pallas import tpu as pltpu
from jax.sharding import PartitionSpec as P

MESH = pl.DeviceIdType.MESH
LANES = 128
F32, BF16 = jnp.float32, jnp.bfloat16


def flip(value, mask, size):
    result, bit = 0, 1
    while bit < size:
        digit = lax.rem(lax.div(value, bit), 2)
        result = result + (1 - digit if (mask // bit) % 2 else digit) * bit
        bit *= 2
    return result


def split(value):
    high = value.astype(BF16)
    return high, (value - high.astype(F32)).astype(BF16)


def dot(a, b):
    return jnp.dot(a, b, preferred_element_type=F32)


def dot3(high, low, right_high, right_low):
    return dot(high, right_high) + (dot(high, right_low) + dot(low, right_high))


def complex_rows(rows, right_high, right_low):
    m = rows.shape[0] // 2
    high, low = split(rows)
    by_real = dot3(high, low, right_high[0], right_low[0])
    by_imag = dot3(high, low, right_high[1], right_low[1])
    return by_real[:m] - by_imag[m:], by_imag[:m] + by_real[m:]


def kernel(n, order_ref, stem_ref, branch_ref, out_ref, last_high, last_low, tail_high, tail_low, stem, xh, xl, bh, bl, dh, dl, wh, wl,
           lch, lcl, sent, got, order, order_sem, stem_sem, left_sem, side_sem, send_sem, recv_sem, notice, left_0, left_1, *branch):
    bw = stem.shape[1]
    rows = bw // n
    per = LANES // rows
    groups = n // per
    me = lax.axis_index("mode")
    z, q = lax.div(me, per), lax.rem(me, per)
    upper = lax.div(q, per // 2)
    sequence = [groups // 2] + [s for s in range(1, groups) if s != groups // 2] + [0]
    early = sequence[: groups // 2]
    lead, last = sequence[0], sequence[-2]

    def column(s):
        return pl.ds(pl.multiple_of(flip(z, s, groups) * LANES, LANES), LANES)

    order_copy = pltpu.make_async_copy(order_ref, order, order_sem)
    order_copy.start()
    halves = [pl.ds(h * (bw // 2), bw // 2) for h in range(2)]
    left = (left_0, left_1)
    left_copies = [pltpu.make_async_copy(
        branch_ref.at[:, :, half, column(lead)], left[h], left_sem.at[h]) for h, half in enumerate(halves)]
    stem_copies = [pltpu.make_async_copy(
        stem_ref.at[:, half, halves[0]], stem.at[:, half, halves[0]], stem_sem.at[k]) for k, half in enumerate(halves)]
    side_copy = pltpu.make_async_copy(stem_ref.at[:, :, halves[1]], stem.at[:, :, halves[1]], side_sem)
    for copy in (left_copies[0], stem_copies[0], left_copies[1], stem_copies[1], side_copy):
        copy.start()
    barrier = pltpu.get_barrier_semaphore()
    top, middle = groups - 1, groups // 2
    near = middle ^ top

    def greet(sem, s, k):
        pl.semaphore_signal(
            sem, inc=1, device_id={"mode": flip(z, s, groups) * per + flip(q, k, per)}, device_id_type=MESH)

    for s in range(groups - 1, -1, -1):
        for k in range(per):
            if s == near:
                pl.when(z != top)(functools.partial(greet, barrier, s, k))
            elif s == lead:
                pl.when(z + upper != top + 1)(functools.partial(greet, barrier, s, k))
            elif s or k:
                greet(barrier, s, k)

    def equal(a, b):
        return (a == b).astype(jnp.int32)

    def enter():
        pl.semaphore_wait(barrier, n - 1 - per * equal(z, middle) - per // 2 * equal(z, middle - 1))
        for k in range(per):
            pl.when(z == top)(functools.partial(greet, notice, near, k))
            pl.when(z + upper == top + 1)(functools.partial(greet, notice, lead, k))

    free = [left_sem.at[0], stem_sem.at[0], left_sem.at[1], stem_sem.at[1]]
    branch_copies = {
        s: pltpu.make_async_copy(branch_ref.at[:, :, :, column(s)], branch[s], sem)
        for s, sem in zip(sequence[1:] + [lead], free)}
    order_copy.wait()
    o0, o1, o2, o3 = (order[k] for k in range(4))

    def left_rows(s):
        return jnp.concatenate([branch[s][o0, part].T for part in range(2)], axis=0)

    def first_rows(s):
        return complex_rows(left_rows(s), xh, xl)

    def partner(s, i):
        if s == lead:
            return i
        if s != last:
            return flip(q, i, per)
        column = upper if i >= per // 2 else 1 - upper
        return column * (per // 2) + (per - 1 - i) % (per // 2)

    def hop(s, i, h=None):
        j = partner(s, i)
        where = () if h is None else (slice(None), slice(None), halves[h])
        return pltpu.make_async_remote_copy(
            src_ref=sent.at[(s * per + j, *where)], dst_ref=got.at[(s, q, *where)], send_sem=send_sem,
            recv_sem=recv_sem.at[groups - 1 + h if s == last else s - (s > last)],
            device_id={"mode": flip(z, s, groups) * per + j}, device_id_type=MESH)

    def await_bytes(place, sem):
        pltpu.make_async_copy(place, place, sem).wait()

    def own(s):
        return pltpu.make_async_copy(sent.at[s * per + q], got.at[s, q], recv_sem.at[s - (s > last)])

    def send(s, real, imag, which=range(per)):
        for place, j in enumerate(which):
            sent[s * per + j, 0] = real[place * rows:(place + 1) * rows]
            sent[s * per + j, 1] = imag[place * rows:(place + 1) * rows]
        for h in range(2) if s == last else [None]:
            for i in which:
                own(s).start() if s == 0 and i == 0 else hop(s, i, h).start()

    highs, lows = [], []
    parcels = [range(per // 2), range(per // 2, per)]
    by = [None, None]

    def send_lead(by, which, h=None):
        m = by[0].shape[0] // 2
        side = slice(None) if h is None else slice(h * (bw // 2), (h + 1) * (bw // 2))
        for part, value in enumerate((by[0][:m] - by[1][m:], by[1][:m] + by[0][m:])):
            for place, j in enumerate(which):
                sent[lead * per + j, part, :, side] = value[place * rows:(place + 1) * rows]
        for j in which:
            hop(lead, j, h).start()

    left_side, right_side = slice(0, bw // 2), slice(bw // 2, bw)
    for k, half in enumerate(halves):
        left_copies[k].wait()
        high, low = split(jnp.concatenate([
            left[k][o0, part].T[which[0] * rows:(which[-1] + 1) * rows] for which in parcels for part in range(2)], axis=0))
        highs.append(high)
        lows.append(low)
        stem_copies[k].wait()
        for part in range(2):
            xh[part, half, left_side], xl[part, half, left_side] = split(stem[part, half, left_side])
            add = dot3(high[:LANES], low[:LANES], xh[part, half, left_side], xl[part, half, left_side])
            by[part] = add if k == 0 else by[part] + add
    enter()
    send_lead(by, parcels[0], 0)
    side_copy.wait()
    for s in sequence[1:] + [lead]:
        branch_copies[s].start()
    for part in range(2):
        xh[part, :, right_side], xl[part, :, right_side] = split(stem[part, :, right_side])
    high, low = (jnp.concatenate([piece[:LANES] for piece in pieces], axis=1) for pieces in (highs, lows))
    send_lead([dot3(high, low, xh[part, :, right_side], xl[part, :, right_side]) for part in range(2)], parcels[0], 1)
    high, low = (jnp.concatenate([piece[LANES:] for piece in pieces], axis=1) for pieces in (highs, lows))
    rest = [dot3(high, low, xh[part], xl[part]) for part in range(2)]
    pl.when(z == middle - 1)(lambda: pl.semaphore_wait(notice, per // 2))
    send_lead(rest, parcels[1])
    for s in early[1:]:
        branch_copies[s].wait()
        if s == near:
            pl.when(z == middle)(lambda: pl.semaphore_wait(notice, per))
        send(s, *first_rows(s))
    for s in sequence[len(early):] + [lead]:
        branch_copies[s].wait()

    for s in range(groups):
        for part in range(2):
            bh[part, :, column(s)], bl[part, :, column(s)] = split(branch[s][o1, part])
            dh[part, :, column(s)], dl[part, :, column(s)] = split(branch[s][o3, part])

    def both(i, carry):
        at = pl.ds(pl.multiple_of(i * LANES, LANES), LANES)
        high = jnp.concatenate([bh[0, at], bh[1, at]], axis=0)
        low = jnp.concatenate([bl[0, at], bl[1, at]], axis=0)
        by_real = dot3(high, low, dh[0], dl[0])
        by_imag = dot3(high, low, dh[1], dl[1])
        wh[0, at], wl[0, at] = split(by_real[:LANES] - by_imag[LANES:])
        wh[1, at], wl[1, at] = split(by_imag[:LANES] + by_real[LANES:])
        return carry

    lax.fori_loop(0, bw // LANES, both, 0)

    for s in sequence[len(early):]:
        real, imag = first_rows(s)
        send(s, *complex_rows(jnp.concatenate([real, imag], axis=0), wh, wl))

    for s in range(groups):
        high_ref, low_ref = (last_high, last_low) if s == last else (lch.at[s], lcl.at[s])
        for t in range(groups):
            real, imag = (split(branch[t][o2, part, column(s), :].T) for part in range(2))
            top = column(t)
            low_half = pl.ds(pl.multiple_of(bw + flip(z, t, groups) * LANES, LANES), LANES)
            for ref, r, i in ((high_ref, real[0], imag[0]), (low_ref, real[1], imag[1])):
                ref[top, :LANES] = r
                ref[top, LANES:] = -i
                ref[low_half, :LANES] = i
                ref[low_half, LANES:] = r

    arrivals = [0] + [s for s in early if s != groups // 2] + [groups // 2] + [s for s in sequence[len(early):] if s]
    tile = 2 * LANES

    def arrived(s, side):
        return jnp.concatenate([got[s, j, part, :, side] for part in range(2) for j in range(per)], axis=0)

    for index, s in enumerate(arrivals):
        if s == last:
            await_bytes(got.at[last, :, :, :, halves[0]], recv_sem.at[groups - 1])
            side = slice(0, bw // 2)
        else:
            await_bytes(got.at[s], recv_sem.at[s - (s > last)])
            side = slice(0, bw)
        right = arrived(s, side)
        if s in early:
            right = jnp.concatenate(complex_rows(right, wh, wl), axis=0)
        right_high, right_low = split(right)
        high_ref, low_ref = (last_high, last_low) if s == last else (lch.at[s], lcl.at[s])
        for i in range(2 * bw // tile):
            at = slice(i * tile, (i + 1) * tile)
            part, row = divmod(i * tile, bw)
            place = (part, slice(row, row + tile), side)
            add = dot3(high_ref[at], low_ref[at], right_high, right_low)
            out_ref[place] = add if index == 0 else out_ref[place] + add
    await_bytes(sent.at[pl.ds(0, n - 1)], send_sem)
    await_bytes(got.at[last, :, :, :, halves[1]], recv_sem.at[groups])
    tail_high[...], tail_low[...] = split(arrived(last, slice(bw // 2, bw)))


def finish(acc_ref, high_ref, low_ref, right_high, right_low, out_ref, tiles, sem):
    count, tile, half = tiles.shape
    ready = pltpu.make_async_copy(acc_ref.at[:, :, pl.ds(0, half)], out_ref.at[:, :, pl.ds(0, half)], sem.at[0])
    ready.start()
    right = right_high[...], right_low[...]
    for i in range(count):
        part, row = divmod(i * tile, 2 * half)
        at = slice(i * tile, (i + 1) * tile)
        tiles[i] = acc_ref[part, row:row + tile, half:] + dot3(high_ref[at], low_ref[at], *right)
        pltpu.make_async_copy(tiles.at[i], out_ref.at[part, pl.ds(row, tile), pl.ds(half, half)], sem.at[1]).start()
    ready.wait()
    pltpu.make_async_copy(tiles, tiles, sem.at[1]).wait()


def fused(n, stem_tensor, branch_tensors, branch_order):
    bw = stem_tensor.shape[-1]
    rows = bw // n
    per = LANES // rows
    groups = n // per
    square = pltpu.VMEM((2, bw, bw), BF16)
    hbm = functools.partial(pltpu.with_memory_space_constraint, memory_space=pltpu.HBM)
    window = pltpu.VMEM((groups, 2 * bw, 2 * LANES), BF16)
    vmem = pl.BlockSpec(memory_space=pltpu.VMEM)
    tiles = 2 * bw // LANES
    partial = pl.pallas_call(
        functools.partial(kernel, n),
        out_shape=[
            jax.ShapeDtypeStruct((2, bw, bw), F32),
            *[jax.ShapeDtypeStruct((2 * bw, 2 * LANES), BF16)] * 2,
            *[jax.ShapeDtypeStruct((2 * LANES, bw // 2), BF16)] * 2,
        ],
        in_specs=[pl.BlockSpec(memory_space=pl.ANY)] * 3,
        out_specs=[vmem] * 5,
        scratch_shapes=[
            pltpu.VMEM((2, bw, bw), F32),
            *[square] * 8,
            window,
            window,
            pltpu.VMEM((n, 2, rows, bw), F32),
            pltpu.VMEM((groups, per, 2, rows, bw), F32),
            pltpu.SMEM(branch_order.shape, jnp.int32),
            pltpu.SemaphoreType.DMA,
            pltpu.SemaphoreType.DMA((2,)),
            pltpu.SemaphoreType.DMA((2,)),
            pltpu.SemaphoreType.DMA,
            pltpu.SemaphoreType.DMA,
            pltpu.SemaphoreType.DMA((groups + 1,)),
            pltpu.SemaphoreType.REGULAR,
            *[pltpu.VMEM((4, 2, bw // 2, LANES), F32)] * 2,
            *[pltpu.VMEM((4, 2, bw, LANES), F32)] * groups,
        ],
        compiler_params=pltpu.CompilerParams(collective_id=0, has_side_effects=True, vmem_limit_bytes=40 << 20),
    )(hbm(branch_order), hbm(stem_tensor.reshape(2, bw, bw)), hbm(branch_tensors))
    return pl.pallas_call(
        finish,
        out_shape=jax.ShapeDtypeStruct((2, bw, bw), F32),
        in_specs=[vmem] * 5,
        out_specs=pl.BlockSpec(memory_space=pl.ANY),
        scratch_shapes=[pltpu.VMEM((tiles, LANES, bw // 2), F32), pltpu.SemaphoreType.DMA((2,))],
        compiler_params=pltpu.CompilerParams(vmem_limit_bytes=8 << 20),
    )(*partial).reshape(stem_tensor.shape)


def complex_product(first, second, form):
    high = lax.Precision.HIGHEST
    real = jnp.einsum(form, first[0], second[0], precision=high) - jnp.einsum(form, first[1], second[1], precision=high)
    imag = jnp.einsum(form, first[0], second[1], precision=high) + jnp.einsum(form, first[1], second[0], precision=high)
    return jnp.stack([real, imag])


def plain(stem_tensor, branch_tensors, branch_order):
    field = stem_tensor[:, :, 0]
    chosen = [branch_tensors[branch_order[index]] for index in range(4)]
    field = complex_product(field, chosen[0], "sce,cd->sde")
    field = complex_product(field, chosen[1], "sce,ed->scd")
    moved = lax.all_to_all(field[:, :, None], "mode", split_axis=3, concat_axis=2, tiled=True)
    merged = moved.reshape(field.shape)
    merged = complex_product(merged, chosen[2], "sce,cd->sde")
    return complex_product(merged, chosen[3], "sce,ed->scd")[:, :, None]


def on_device(n, stem_tensor, branch_tensors, branch_order):
    _, stems, held, bw, _ = stem_tensor.shape
    rows = bw // n
    fits = stems == held == 1 and rows % 8 == 0 and 3 * rows <= LANES and n & (n - 1) == 0 and n * rows == bw
    if fits and bw % (4 * LANES) == 0:
        return fused(n, stem_tensor, branch_tensors, branch_order)
    return plain(stem_tensor, branch_tensors, branch_order)


def solution(mesh):
    return jax.shard_map(
        functools.partial(on_device, mesh.shape["mode"]),
        mesh=mesh,
        in_specs=(P(None, "cuts", "mode", None, None), P(), P()),
        out_specs=P(None, "cuts", "mode", None, None),
        check_vma=False,
    )
```

```python
import functools

import jax
import jax.numpy as jnp
from jax import lax
from jax.experimental import pallas as pl
from jax.experimental.pallas import tpu as pltpu
from jax.sharding import PartitionSpec as P

MESH = pl.DeviceIdType.MESH
LANES = 128
F32, BF16 = jnp.float32, jnp.bfloat16


def flip(value, mask, size):
    result, bit = 0, 1
    while bit < size:
        digit = lax.rem(lax.div(value, bit), 2)
        result = result + (1 - digit if (mask // bit) % 2 else digit) * bit
        bit *= 2
    return result


def split(value):
    high = value.astype(BF16)
    return high, (value - high.astype(F32)).astype(BF16)


def dot(a, b):
    return jnp.dot(a, b, preferred_element_type=F32)


def dot3(high, low, right_high, right_low):
    return dot(high, right_high) + (dot(high, right_low) + dot(low, right_high))


def complex_rows(rows, right_high, right_low):
    m = rows.shape[0] // 2
    high, low = split(rows)
    by_real = dot3(high, low, right_high[0], right_low[0])
    by_imag = dot3(high, low, right_high[1], right_low[1])
    return by_real[:m] - by_imag[m:], by_imag[:m] + by_real[m:]


def kernel(n, order_ref, stem_ref, branch_ref, out_ref, last_high, last_low, tail_high, tail_low, stem, xh, xl, bh, bl, dh, dl, wh, wl,
           lch, lcl, sent, got, order, order_sem, stem_sem, left_sem, side_sem, send_sem, recv_sem, notice, left_0, left_1, *branch):
    bw = stem.shape[1]
    rows = bw // n
    per = LANES // rows
    groups = n // per
    me = lax.axis_index("mode")
    z, q = lax.div(me, per), lax.rem(me, per)
    upper = lax.div(q, per // 2)
    sequence = [groups // 2] + [s for s in range(1, groups) if s != groups // 2] + [0]
    early = sequence[: groups // 2]
    lead, last = sequence[0], sequence[-2]

    def column(s):
        return pl.ds(pl.multiple_of(flip(z, s, groups) * LANES, LANES), LANES)

    order_copy = pltpu.make_async_copy(order_ref, order, order_sem)
    order_copy.start()
    halves = [pl.ds(h * (bw // 2), bw // 2) for h in range(2)]
    left = (left_0, left_1)
    left_copies = [pltpu.make_async_copy(
        branch_ref.at[:, :, half, column(lead)], left[h], left_sem.at[h]) for h, half in enumerate(halves)]
    stem_copies = [pltpu.make_async_copy(
        stem_ref.at[:, half, halves[0]], stem.at[:, half, halves[0]], stem_sem.at[k]) for k, half in enumerate(halves)]
    side_copy = pltpu.make_async_copy(stem_ref.at[:, :, halves[1]], stem.at[:, :, halves[1]], side_sem)
    for copy in (left_copies[0], stem_copies[0], left_copies[1], stem_copies[1], side_copy):
        copy.start()
    barrier = pltpu.get_barrier_semaphore()
    top, middle = groups - 1, groups // 2
    near = middle ^ top

    def greet(sem, s, k):
        pl.semaphore_signal(
            sem, inc=1, device_id={"mode": flip(z, s, groups) * per + flip(q, k, per)}, device_id_type=MESH)

    for s in range(groups - 1, -1, -1):
        for k in range(per):
            if s == near:
                pl.when(z != top)(functools.partial(greet, barrier, s, k))
            elif s == lead:
                pl.when(z + upper != top + 1)(functools.partial(greet, barrier, s, k))
            elif s or k:
                greet(barrier, s, k)

    def equal(a, b):
        return (a == b).astype(jnp.int32)

    def enter():
        pl.semaphore_wait(barrier, n - 1 - per * equal(z, middle) - per // 2 * equal(z, middle - 1))

    def announce():
        for k in range(per):
            pl.when(z == top)(functools.partial(greet, notice, near, k))
            pl.when(z + upper == top + 1)(functools.partial(greet, notice, lead, k))

    free = [left_sem.at[0], stem_sem.at[0], left_sem.at[1], stem_sem.at[1]]
    branch_copies = {
        s: pltpu.make_async_copy(branch_ref.at[:, :, :, column(s)], branch[s], sem)
        for s, sem in zip(sequence[1:] + [lead], free)}
    order_copy.wait()
    o0, o1, o2, o3 = (order[k] for k in range(4))

    def left_rows(s):
        return jnp.concatenate([branch[s][o0, part].T for part in range(2)], axis=0)

    def first_rows(s):
        return complex_rows(left_rows(s), xh, xl)

    def partner(s, i):
        if s == lead:
            return i
        if s != last:
            return flip(q, i, per)
        column = upper if i >= per // 2 else 1 - upper
        return column * (per // 2) + (per - 1 - i) % (per // 2)

    def hop(s, i, h=None):
        j = partner(s, i)
        where = () if h is None else (slice(None), slice(None), halves[h])
        return pltpu.make_async_remote_copy(
            src_ref=sent.at[(s * per + j, *where)], dst_ref=got.at[(s, q, *where)], send_sem=send_sem,
            recv_sem=recv_sem.at[groups - 1 + h if s == last else s - (s > last)],
            device_id={"mode": flip(z, s, groups) * per + j}, device_id_type=MESH)

    def await_bytes(place, sem):
        pltpu.make_async_copy(place, place, sem).wait()

    def own(s):
        return pltpu.make_async_copy(sent.at[s * per + q], got.at[s, q], recv_sem.at[s - (s > last)])

    def send(s, real, imag, which=range(per)):
        for place, j in enumerate(which):
            sent[s * per + j, 0] = real[place * rows:(place + 1) * rows]
            sent[s * per + j, 1] = imag[place * rows:(place + 1) * rows]
        for h in range(2) if s == last else [None]:
            for i in which:
                own(s).start() if s == 0 and i == 0 else hop(s, i, h).start()

    highs, lows = [], []
    parcels = [range(per // 2), range(per // 2, per)]
    by = [None, None]

    def send_lead(by, which, h=None):
        m = by[0].shape[0] // 2
        side = slice(None) if h is None else slice(h * (bw // 2), (h + 1) * (bw // 2))
        for part, value in enumerate((by[0][:m] - by[1][m:], by[1][:m] + by[0][m:])):
            for place, j in enumerate(which):
                sent[lead * per + j, part, :, side] = value[place * rows:(place + 1) * rows]
        for j in which:
            hop(lead, j, h).start()

    left_side, right_side = slice(0, bw // 2), slice(bw // 2, bw)
    for k, half in enumerate(halves):
        left_copies[k].wait()
        high, low = split(jnp.concatenate([
            left[k][o0, part].T[which[0] * rows:(which[-1] + 1) * rows] for which in parcels for part in range(2)], axis=0))
        highs.append(high)
        lows.append(low)
        stem_copies[k].wait()
        for part in range(2):
            xh[part, half, left_side], xl[part, half, left_side] = split(stem[part, half, left_side])
            add = dot3(high[:LANES], low[:LANES], xh[part, half, left_side], xl[part, half, left_side])
            by[part] = add if k == 0 else by[part] + add
    enter()
    send_lead(by, parcels[0], 0)
    announce()
    side_copy.wait()
    for s in sequence[1:] + [lead]:
        branch_copies[s].start()
    for part in range(2):
        xh[part, :, right_side], xl[part, :, right_side] = split(stem[part, :, right_side])
    high, low = (jnp.concatenate([piece[:LANES] for piece in pieces], axis=1) for pieces in (highs, lows))
    send_lead([dot3(high, low, xh[part, :, right_side], xl[part, :, right_side]) for part in range(2)], parcels[0], 1)
    high, low = (jnp.concatenate([piece[LANES:] for piece in pieces], axis=1) for pieces in (highs, lows))
    rest = [dot3(high, low, xh[part], xl[part]) for part in range(2)]
    pl.when(z == middle - 1)(lambda: pl.semaphore_wait(notice, per // 2))
    send_lead(rest, parcels[1])
    for s in early[1:]:
        branch_copies[s].wait()
        if s == near:
            pl.when(z == middle)(lambda: pl.semaphore_wait(notice, per))
        send(s, *first_rows(s))
    for s in sequence[len(early):] + [lead]:
        branch_copies[s].wait()

    for s in range(groups):
        for part in range(2):
            bh[part, :, column(s)], bl[part, :, column(s)] = split(branch[s][o1, part])
            dh[part, :, column(s)], dl[part, :, column(s)] = split(branch[s][o3, part])

    def both(i, carry):
        at = pl.ds(pl.multiple_of(i * LANES, LANES), LANES)
        high = jnp.concatenate([bh[0, at], bh[1, at]], axis=0)
        low = jnp.concatenate([bl[0, at], bl[1, at]], axis=0)
        by_real = dot3(high, low, dh[0], dl[0])
        by_imag = dot3(high, low, dh[1], dl[1])
        wh[0, at], wl[0, at] = split(by_real[:LANES] - by_imag[LANES:])
        wh[1, at], wl[1, at] = split(by_imag[:LANES] + by_real[LANES:])
        return carry

    lax.fori_loop(0, bw // LANES, both, 0)

    for s in sequence[len(early):]:
        real, imag = first_rows(s)
        send(s, *complex_rows(jnp.concatenate([real, imag], axis=0), wh, wl))

    for s in range(groups):
        high_ref, low_ref = (last_high, last_low) if s == last else (lch.at[s], lcl.at[s])
        for t in range(groups):
            real, imag = (split(branch[t][o2, part, column(s), :].T) for part in range(2))
            top = column(t)
            low_half = pl.ds(pl.multiple_of(bw + flip(z, t, groups) * LANES, LANES), LANES)
            for ref, r, i in ((high_ref, real[0], imag[0]), (low_ref, real[1], imag[1])):
                ref[top, :LANES] = r
                ref[top, LANES:] = -i
                ref[low_half, :LANES] = i
                ref[low_half, LANES:] = r

    arrivals = [0] + [s for s in early if s != groups // 2] + [groups // 2] + [s for s in sequence[len(early):] if s]
    tile = 2 * LANES

    def arrived(s, side):
        return jnp.concatenate([got[s, j, part, :, side] for part in range(2) for j in range(per)], axis=0)

    for index, s in enumerate(arrivals):
        if s == last:
            await_bytes(got.at[last, :, :, :, halves[0]], recv_sem.at[groups - 1])
            side = slice(0, bw // 2)
        else:
            await_bytes(got.at[s], recv_sem.at[s - (s > last)])
            side = slice(0, bw)
        right = arrived(s, side)
        if s in early:
            right = jnp.concatenate(complex_rows(right, wh, wl), axis=0)
        right_high, right_low = split(right)
        high_ref, low_ref = (last_high, last_low) if s == last else (lch.at[s], lcl.at[s])
        for i in range(2 * bw // tile):
            at = slice(i * tile, (i + 1) * tile)
            part, row = divmod(i * tile, bw)
            place = (part, slice(row, row + tile), side)
            add = dot3(high_ref[at], low_ref[at], right_high, right_low)
            out_ref[place] = add if index == 0 else out_ref[place] + add
    await_bytes(sent.at[pl.ds(0, n - 1)], send_sem)
    await_bytes(got.at[last, :, :, :, halves[1]], recv_sem.at[groups])
    tail_high[...], tail_low[...] = split(arrived(last, slice(bw // 2, bw)))


def finish(acc_ref, high_ref, low_ref, right_high, right_low, out_ref, tiles, sem):
    count, tile, half = tiles.shape
    ready = pltpu.make_async_copy(acc_ref.at[:, :, pl.ds(0, half)], out_ref.at[:, :, pl.ds(0, half)], sem.at[0])
    ready.start()
    right = right_high[...], right_low[...]
    for i in range(count):
        part, row = divmod(i * tile, 2 * half)
        at = slice(i * tile, (i + 1) * tile)
        tiles[i] = acc_ref[part, row:row + tile, half:] + dot3(high_ref[at], low_ref[at], *right)
        pltpu.make_async_copy(tiles.at[i], out_ref.at[part, pl.ds(row, tile), pl.ds(half, half)], sem.at[1]).start()
    ready.wait()
    pltpu.make_async_copy(tiles, tiles, sem.at[1]).wait()


def fused(n, stem_tensor, branch_tensors, branch_order):
    bw = stem_tensor.shape[-1]
    rows = bw // n
    per = LANES // rows
    groups = n // per
    square = pltpu.VMEM((2, bw, bw), BF16)
    hbm = functools.partial(pltpu.with_memory_space_constraint, memory_space=pltpu.HBM)
    window = pltpu.VMEM((groups, 2 * bw, 2 * LANES), BF16)
    vmem = pl.BlockSpec(memory_space=pltpu.VMEM)
    tiles = 2 * bw // LANES
    partial = pl.pallas_call(
        functools.partial(kernel, n),
        out_shape=[
            jax.ShapeDtypeStruct((2, bw, bw), F32),
            *[jax.ShapeDtypeStruct((2 * bw, 2 * LANES), BF16)] * 2,
            *[jax.ShapeDtypeStruct((2 * LANES, bw // 2), BF16)] * 2,
        ],
        in_specs=[pl.BlockSpec(memory_space=pl.ANY)] * 3,
        out_specs=[vmem] * 5,
        scratch_shapes=[
            pltpu.VMEM((2, bw, bw), F32),
            *[square] * 8,
            window,
            window,
            pltpu.VMEM((n, 2, rows, bw), F32),
            pltpu.VMEM((groups, per, 2, rows, bw), F32),
            pltpu.SMEM(branch_order.shape, jnp.int32),
            pltpu.SemaphoreType.DMA,
            pltpu.SemaphoreType.DMA((2,)),
            pltpu.SemaphoreType.DMA((2,)),
            pltpu.SemaphoreType.DMA,
            pltpu.SemaphoreType.DMA,
            pltpu.SemaphoreType.DMA((groups + 1,)),
            pltpu.SemaphoreType.REGULAR,
            *[pltpu.VMEM((4, 2, bw // 2, LANES), F32)] * 2,
            *[pltpu.VMEM((4, 2, bw, LANES), F32)] * groups,
        ],
        compiler_params=pltpu.CompilerParams(collective_id=0, has_side_effects=True, vmem_limit_bytes=40 << 20),
    )(hbm(branch_order), hbm(stem_tensor.reshape(2, bw, bw)), hbm(branch_tensors))
    return pl.pallas_call(
        finish,
        out_shape=jax.ShapeDtypeStruct((2, bw, bw), F32),
        in_specs=[vmem] * 5,
        out_specs=pl.BlockSpec(memory_space=pl.ANY),
        scratch_shapes=[pltpu.VMEM((tiles, LANES, bw // 2), F32), pltpu.SemaphoreType.DMA((2,))],
        compiler_params=pltpu.CompilerParams(vmem_limit_bytes=8 << 20),
    )(*partial).reshape(stem_tensor.shape)


def complex_product(first, second, form):
    high = lax.Precision.HIGHEST
    real = jnp.einsum(form, first[0], second[0], precision=high) - jnp.einsum(form, first[1], second[1], precision=high)
    imag = jnp.einsum(form, first[0], second[1], precision=high) + jnp.einsum(form, first[1], second[0], precision=high)
    return jnp.stack([real, imag])


def plain(stem_tensor, branch_tensors, branch_order):
    field = stem_tensor[:, :, 0]
    chosen = [branch_tensors[branch_order[index]] for index in range(4)]
    field = complex_product(field, chosen[0], "sce,cd->sde")
    field = complex_product(field, chosen[1], "sce,ed->scd")
    moved = lax.all_to_all(field[:, :, None], "mode", split_axis=3, concat_axis=2, tiled=True)
    merged = moved.reshape(field.shape)
    merged = complex_product(merged, chosen[2], "sce,cd->sde")
    return complex_product(merged, chosen[3], "sce,ed->scd")[:, :, None]


def on_device(n, stem_tensor, branch_tensors, branch_order):
    _, stems, held, bw, _ = stem_tensor.shape
    rows = bw // n
    fits = stems == held == 1 and rows % 8 == 0 and 3 * rows <= LANES and n & (n - 1) == 0 and n * rows == bw
    if fits and bw % (4 * LANES) == 0:
        return fused(n, stem_tensor, branch_tensors, branch_order)
    return plain(stem_tensor, branch_tensors, branch_order)


def solution(mesh):
    return jax.shard_map(
        functools.partial(on_device, mesh.shape["mode"]),
        mesh=mesh,
        in_specs=(P(None, "cuts", "mode", None, None), P(), P()),
        out_specs=P(None, "cuts", "mode", None, None),
        check_vma=False,
    )
```

```python
import functools

import jax
import jax.numpy as jnp
from jax import lax
from jax.experimental import pallas as pl
from jax.experimental.pallas import tpu as pltpu
from jax.sharding import PartitionSpec as P

MESH = pl.DeviceIdType.MESH
LANES = 128
F32, BF16 = jnp.float32, jnp.bfloat16


def flip(value, mask, size):
    result, bit = 0, 1
    while bit < size:
        digit = lax.rem(lax.div(value, bit), 2)
        result = result + (1 - digit if (mask // bit) % 2 else digit) * bit
        bit *= 2
    return result


def split(value):
    high = value.astype(BF16)
    return high, (value - high.astype(F32)).astype(BF16)


def dot(a, b):
    return jnp.dot(a, b, preferred_element_type=F32)


def dot3(high, low, right_high, right_low):
    return dot(high, right_high) + (dot(high, right_low) + dot(low, right_high))


def complex_rows(rows, right_high, right_low):
    m = rows.shape[0] // 2
    high, low = split(rows)
    by_real = dot3(high, low, right_high[0], right_low[0])
    by_imag = dot3(high, low, right_high[1], right_low[1])
    return by_real[:m] - by_imag[m:], by_imag[:m] + by_real[m:]


def kernel(n, order_ref, stem_ref, branch_ref, out_ref, last_high, last_low, tail_high, tail_low, stem, xh, xl, bh, bl, dh, dl, wh, wl,
           lch, lcl, sent, got, order, order_sem, stem_sem, left_sem, side_sem, send_sem, recv_sem, notice, left_0, left_1, *branch):
    bw = stem.shape[1]
    rows = bw // n
    per = LANES // rows
    groups = n // per
    me = lax.axis_index("mode")
    z, q = lax.div(me, per), lax.rem(me, per)
    upper = lax.div(q, per // 2)
    sequence = [groups // 2] + [s for s in range(1, groups) if s != groups // 2] + [0]
    early = sequence[: groups // 2]
    lead, last = sequence[0], sequence[-2]

    def column(s):
        return pl.ds(pl.multiple_of(flip(z, s, groups) * LANES, LANES), LANES)

    order_copy = pltpu.make_async_copy(order_ref, order, order_sem)
    order_copy.start()
    halves = [pl.ds(h * (bw // 2), bw // 2) for h in range(2)]
    ends = [pl.ds(0, bw - LANES), pl.ds(bw - LANES, LANES)]
    left = (left_0, left_1)
    left_copies = [pltpu.make_async_copy(
        branch_ref.at[:, :, half, column(lead)], left[h], left_sem.at[h]) for h, half in enumerate(halves)]
    stem_copies = [pltpu.make_async_copy(
        stem_ref.at[:, half, halves[0]], stem.at[:, half, halves[0]], stem_sem.at[k]) for k, half in enumerate(halves)]
    side_copy = pltpu.make_async_copy(stem_ref.at[:, :, halves[1]], stem.at[:, :, halves[1]], side_sem)
    for copy in (left_copies[0], stem_copies[0], left_copies[1], stem_copies[1], side_copy):
        copy.start()
    barrier = pltpu.get_barrier_semaphore()
    top, middle = groups - 1, groups // 2
    near = middle ^ top

    def greet(sem, s, k):
        pl.semaphore_signal(
            sem, inc=1, device_id={"mode": flip(z, s, groups) * per + flip(q, k, per)}, device_id_type=MESH)

    for s in range(groups - 1, -1, -1):
        for k in range(per):
            if s == near:
                pl.when(z != top)(functools.partial(greet, barrier, s, k))
            elif s == lead:
                pl.when(z + upper != top + 1)(functools.partial(greet, barrier, s, k))
            elif s or k:
                greet(barrier, s, k)

    def equal(a, b):
        return (a == b).astype(jnp.int32)

    def enter():
        pl.semaphore_wait(barrier, n - 1 - per * equal(z, middle) - per // 2 * equal(z, middle - 1))
        for k in range(per):
            pl.when(z == top)(functools.partial(greet, notice, near, k))
            pl.when(z + upper == top + 1)(functools.partial(greet, notice, lead, k))

    free = [left_sem.at[0], stem_sem.at[0], left_sem.at[1], stem_sem.at[1]]
    branch_copies = {
        s: pltpu.make_async_copy(branch_ref.at[:, :, :, column(s)], branch[s], sem)
        for s, sem in zip(sequence[1:] + [lead], free)}
    order_copy.wait()
    o0, o1, o2, o3 = (order[k] for k in range(4))

    def left_rows(s):
        return jnp.concatenate([branch[s][o0, part].T for part in range(2)], axis=0)

    def first_rows(s):
        return complex_rows(left_rows(s), xh, xl)

    def partner(s, i):
        if s == lead:
            return i
        if s != last:
            return flip(q, i, per)
        column = upper if i >= per // 2 else 1 - upper
        return column * (per // 2) + (per - 1 - i) % (per // 2)

    def hop(s, i, h=None):
        j = partner(s, i)
        where = () if h is None else (slice(None), slice(None), (ends if s == last else halves)[h])
        return pltpu.make_async_remote_copy(
            src_ref=sent.at[(s * per + j, *where)], dst_ref=got.at[(s, q, *where)], send_sem=send_sem,
            recv_sem=recv_sem.at[groups - 1 + h if s == last else s - (s > last)],
            device_id={"mode": flip(z, s, groups) * per + j}, device_id_type=MESH)

    def await_bytes(place, sem):
        pltpu.make_async_copy(place, place, sem).wait()

    def own(s):
        return pltpu.make_async_copy(sent.at[s * per + q], got.at[s, q], recv_sem.at[s - (s > last)])

    def send(s, real, imag, which=range(per)):
        for place, j in enumerate(which):
            sent[s * per + j, 0] = real[place * rows:(place + 1) * rows]
            sent[s * per + j, 1] = imag[place * rows:(place + 1) * rows]
        for h in range(2) if s == last else [None]:
            for i in which:
                own(s).start() if s == 0 and i == 0 else hop(s, i, h).start()

    highs, lows = [], []
    parcels = [range(per // 2), range(per // 2, per)]
    by = [None, None]

    def send_lead(by, which, h=None):
        m = by[0].shape[0] // 2
        side = slice(None) if h is None else slice(h * (bw // 2), (h + 1) * (bw // 2))
        for part, value in enumerate((by[0][:m] - by[1][m:], by[1][:m] + by[0][m:])):
            for place, j in enumerate(which):
                sent[lead * per + j, part, :, side] = value[place * rows:(place + 1) * rows]
        for j in which:
            hop(lead, j, h).start()

    left_side, right_side = slice(0, bw // 2), slice(bw // 2, bw)
    for k, half in enumerate(halves):
        left_copies[k].wait()
        high, low = split(jnp.concatenate([
            left[k][o0, part].T[which[0] * rows:(which[-1] + 1) * rows] for which in parcels for part in range(2)], axis=0))
        highs.append(high)
        lows.append(low)
        stem_copies[k].wait()
        for part in range(2):
            xh[part, half, left_side], xl[part, half, left_side] = split(stem[part, half, left_side])
            add = dot3(high[:LANES], low[:LANES], xh[part, half, left_side], xl[part, half, left_side])
            by[part] = add if k == 0 else by[part] + add
    enter()
    send_lead(by, parcels[0], 0)
    side_copy.wait()
    for s in sequence[1:] + [lead]:
        branch_copies[s].start()
    for part in range(2):
        xh[part, :, right_side], xl[part, :, right_side] = split(stem[part, :, right_side])
    high, low = (jnp.concatenate([piece[:LANES] for piece in pieces], axis=1) for pieces in (highs, lows))
    send_lead([dot3(high, low, xh[part, :, right_side], xl[part, :, right_side]) for part in range(2)], parcels[0], 1)
    high, low = (jnp.concatenate([piece[LANES:] for piece in pieces], axis=1) for pieces in (highs, lows))
    rest = [dot3(high, low, xh[part], xl[part]) for part in range(2)]
    pl.when(z == middle - 1)(lambda: pl.semaphore_wait(notice, per // 2))
    send_lead(rest, parcels[1])
    for s in early[1:]:
        branch_copies[s].wait()
        if s == near:
            pl.when(z == middle)(lambda: pl.semaphore_wait(notice, per))
        send(s, *first_rows(s))
    for s in sequence[len(early):] + [lead]:
        branch_copies[s].wait()

    for s in range(groups):
        for part in range(2):
            bh[part, :, column(s)], bl[part, :, column(s)] = split(branch[s][o1, part])
            dh[part, :, column(s)], dl[part, :, column(s)] = split(branch[s][o3, part])

    def both(i, carry):
        at = pl.ds(pl.multiple_of(i * LANES, LANES), LANES)
        high = jnp.concatenate([bh[0, at], bh[1, at]], axis=0)
        low = jnp.concatenate([bl[0, at], bl[1, at]], axis=0)
        by_real = dot3(high, low, dh[0], dl[0])
        by_imag = dot3(high, low, dh[1], dl[1])
        wh[0, at], wl[0, at] = split(by_real[:LANES] - by_imag[LANES:])
        wh[1, at], wl[1, at] = split(by_imag[:LANES] + by_real[LANES:])
        return carry

    lax.fori_loop(0, bw // LANES, both, 0)

    for s in sequence[len(early):]:
        real, imag = first_rows(s)
        send(s, *complex_rows(jnp.concatenate([real, imag], axis=0), wh, wl))

    for s in range(groups):
        high_ref, low_ref = (last_high, last_low) if s == last else (lch.at[s], lcl.at[s])
        for t in range(groups):
            real, imag = (split(branch[t][o2, part, column(s), :].T) for part in range(2))
            top = column(t)
            low_half = pl.ds(pl.multiple_of(bw + flip(z, t, groups) * LANES, LANES), LANES)
            for ref, r, i in ((high_ref, real[0], imag[0]), (low_ref, real[1], imag[1])):
                ref[top, :LANES] = r
                ref[top, LANES:] = -i
                ref[low_half, :LANES] = i
                ref[low_half, LANES:] = r

    arrivals = [0] + [s for s in early if s != groups // 2] + [groups // 2] + [s for s in sequence[len(early):] if s]
    tile = 2 * LANES

    def arrived(s, side):
        return jnp.concatenate([got[s, j, part, :, side] for part in range(2) for j in range(per)], axis=0)

    for index, s in enumerate(arrivals):
        if s == last:
            await_bytes(got.at[last, :, :, :, ends[0]], recv_sem.at[groups - 1])
            side = slice(0, bw - LANES)
        else:
            await_bytes(got.at[s], recv_sem.at[s - (s > last)])
            side = slice(0, bw)
        right = arrived(s, side)
        if s in early:
            right = jnp.concatenate(complex_rows(right, wh, wl), axis=0)
        right_high, right_low = split(right)
        high_ref, low_ref = (last_high, last_low) if s == last else (lch.at[s], lcl.at[s])
        for i in range(2 * bw // tile):
            at = slice(i * tile, (i + 1) * tile)
            part, row = divmod(i * tile, bw)
            place = (part, slice(row, row + tile), side)
            add = dot3(high_ref[at], low_ref[at], right_high, right_low)
            out_ref[place] = add if index == 0 else out_ref[place] + add
    await_bytes(sent.at[pl.ds(0, n - 1)], send_sem)
    await_bytes(got.at[last, :, :, :, ends[1]], recv_sem.at[groups])
    tail_high[...], tail_low[...] = split(arrived(last, slice(bw - LANES, bw)))


def finish(acc_ref, high_ref, low_ref, right_high, right_low, out_ref, tiles, sem):
    count, tile, width = tiles.shape
    bw = acc_ref.shape[-1]
    begin = bw - width
    ready = pltpu.make_async_copy(acc_ref.at[:, :, pl.ds(0, begin)], out_ref.at[:, :, pl.ds(0, begin)], sem.at[0])
    ready.start()
    right = right_high[...], right_low[...]
    for i in range(count):
        part, row = divmod(i * tile, bw)
        at = slice(i * tile, (i + 1) * tile)
        tiles[i] = acc_ref[part, row:row + tile, begin:] + dot3(high_ref[at], low_ref[at], *right)
        pltpu.make_async_copy(tiles.at[i], out_ref.at[part, pl.ds(row, tile), pl.ds(begin, width)], sem.at[1]).start()
    ready.wait()
    pltpu.make_async_copy(tiles, tiles, sem.at[1]).wait()


def fused(n, stem_tensor, branch_tensors, branch_order):
    bw = stem_tensor.shape[-1]
    rows = bw // n
    per = LANES // rows
    groups = n // per
    square = pltpu.VMEM((2, bw, bw), BF16)
    hbm = functools.partial(pltpu.with_memory_space_constraint, memory_space=pltpu.HBM)
    window = pltpu.VMEM((groups, 2 * bw, 2 * LANES), BF16)
    vmem = pl.BlockSpec(memory_space=pltpu.VMEM)
    tiles = bw // LANES
    partial = pl.pallas_call(
        functools.partial(kernel, n),
        out_shape=[
            jax.ShapeDtypeStruct((2, bw, bw), F32),
            *[jax.ShapeDtypeStruct((2 * bw, 2 * LANES), BF16)] * 2,
            *[jax.ShapeDtypeStruct((2 * LANES, LANES), BF16)] * 2,
        ],
        in_specs=[pl.BlockSpec(memory_space=pl.ANY)] * 3,
        out_specs=[vmem] * 5,
        scratch_shapes=[
            pltpu.VMEM((2, bw, bw), F32),
            *[square] * 8,
            window,
            window,
            pltpu.VMEM((n, 2, rows, bw), F32),
            pltpu.VMEM((groups, per, 2, rows, bw), F32),
            pltpu.SMEM(branch_order.shape, jnp.int32),
            pltpu.SemaphoreType.DMA,
            pltpu.SemaphoreType.DMA((2,)),
            pltpu.SemaphoreType.DMA((2,)),
            pltpu.SemaphoreType.DMA,
            pltpu.SemaphoreType.DMA,
            pltpu.SemaphoreType.DMA((groups + 1,)),
            pltpu.SemaphoreType.REGULAR,
            *[pltpu.VMEM((4, 2, bw // 2, LANES), F32)] * 2,
            *[pltpu.VMEM((4, 2, bw, LANES), F32)] * groups,
        ],
        compiler_params=pltpu.CompilerParams(collective_id=0, has_side_effects=True, vmem_limit_bytes=40 << 20),
    )(hbm(branch_order), hbm(stem_tensor.reshape(2, bw, bw)), hbm(branch_tensors))
    return pl.pallas_call(
        finish,
        out_shape=jax.ShapeDtypeStruct((2, bw, bw), F32),
        in_specs=[vmem] * 5,
        out_specs=pl.BlockSpec(memory_space=pl.ANY),
        scratch_shapes=[pltpu.VMEM((tiles, 2 * LANES, LANES), F32), pltpu.SemaphoreType.DMA((2,))],
        compiler_params=pltpu.CompilerParams(vmem_limit_bytes=8 << 20),
    )(*partial).reshape(stem_tensor.shape)


def complex_product(first, second, form):
    high = lax.Precision.HIGHEST
    real = jnp.einsum(form, first[0], second[0], precision=high) - jnp.einsum(form, first[1], second[1], precision=high)
    imag = jnp.einsum(form, first[0], second[1], precision=high) + jnp.einsum(form, first[1], second[0], precision=high)
    return jnp.stack([real, imag])


def plain(stem_tensor, branch_tensors, branch_order):
    field = stem_tensor[:, :, 0]
    chosen = [branch_tensors[branch_order[index]] for index in range(4)]
    field = complex_product(field, chosen[0], "sce,cd->sde")
    field = complex_product(field, chosen[1], "sce,ed->scd")
    moved = lax.all_to_all(field[:, :, None], "mode", split_axis=3, concat_axis=2, tiled=True)
    merged = moved.reshape(field.shape)
    merged = complex_product(merged, chosen[2], "sce,cd->sde")
    return complex_product(merged, chosen[3], "sce,ed->scd")[:, :, None]


def on_device(n, stem_tensor, branch_tensors, branch_order):
    _, stems, held, bw, _ = stem_tensor.shape
    rows = bw // n
    fits = stems == held == 1 and rows % 8 == 0 and 3 * rows <= LANES and n & (n - 1) == 0 and n * rows == bw
    if fits and bw % (4 * LANES) == 0:
        return fused(n, stem_tensor, branch_tensors, branch_order)
    return plain(stem_tensor, branch_tensors, branch_order)


def solution(mesh):
    return jax.shard_map(
        functools.partial(on_device, mesh.shape["mode"]),
        mesh=mesh,
        in_specs=(P(None, "cuts", "mode", None, None), P(), P()),
        out_specs=P(None, "cuts", "mode", None, None),
        check_vma=False,
    )
```

```python
import functools

import jax
import jax.numpy as jnp
from jax import lax
from jax.experimental import pallas as pl
from jax.experimental.pallas import tpu as pltpu
from jax.sharding import PartitionSpec as P

MESH = pl.DeviceIdType.MESH
LANES = 128
F32, BF16 = jnp.float32, jnp.bfloat16


def flip(value, mask, size):
    result, bit = 0, 1
    while bit < size:
        digit = lax.rem(lax.div(value, bit), 2)
        result = result + (1 - digit if (mask // bit) % 2 else digit) * bit
        bit *= 2
    return result


def split(value):
    high = value.astype(BF16)
    return high, (value - high.astype(F32)).astype(BF16)


def dot(a, b):
    return jnp.dot(a, b, preferred_element_type=F32)


def dot3(high, low, right_high, right_low):
    return dot(high, right_high) + (dot(high, right_low) + dot(low, right_high))


def complex_rows(rows, right_high, right_low):
    m = rows.shape[0] // 2
    high, low = split(rows)
    by_real = dot3(high, low, right_high[0], right_low[0])
    by_imag = dot3(high, low, right_high[1], right_low[1])
    return by_real[:m] - by_imag[m:], by_imag[:m] + by_real[m:]


def kernel(n, order_ref, stem_ref, branch_ref, out_ref, last_high, last_low, tail_high, tail_low, stem, xh, xl, bh, bl, dh, dl, wh, wl,
           lch, lcl, sent, got, order, order_sem, stem_sem, left_sem, side_sem, send_sem, recv_sem, notice, left_0, left_1, *branch):
    bw = stem.shape[1]
    rows = bw // n
    per = LANES // rows
    groups = n // per
    me = lax.axis_index("mode")
    z, q = lax.div(me, per), lax.rem(me, per)
    upper = lax.div(q, per // 2)
    sequence = [groups // 2] + [s for s in range(1, groups) if s != groups // 2] + [0]
    early = sequence[: groups // 2]
    lead, last = sequence[0], sequence[-2]

    def column(s):
        return pl.ds(pl.multiple_of(flip(z, s, groups) * LANES, LANES), LANES)

    order_copy = pltpu.make_async_copy(order_ref, order, order_sem)
    order_copy.start()
    halves = [pl.ds(h * (bw // 2), bw // 2) for h in range(2)]
    left = (left_0, left_1)
    left_copies = [pltpu.make_async_copy(
        branch_ref.at[:, :, half, column(lead)], left[h], left_sem.at[h]) for h, half in enumerate(halves)]
    stem_copies = [pltpu.make_async_copy(
        stem_ref.at[:, half, halves[0]], stem.at[:, half, halves[0]], stem_sem.at[k]) for k, half in enumerate(halves)]
    side_copy = pltpu.make_async_copy(stem_ref.at[:, :, halves[1]], stem.at[:, :, halves[1]], side_sem)
    for copy in (left_copies[0], stem_copies[0], left_copies[1], stem_copies[1], side_copy):
        copy.start()
    barrier = pltpu.get_barrier_semaphore()
    top, middle = groups - 1, groups // 2
    near = middle ^ top

    def greet(sem, s, k):
        pl.semaphore_signal(
            sem, inc=1, device_id={"mode": flip(z, s, groups) * per + flip(q, k, per)}, device_id_type=MESH)

    def later(s, k):
        if s == near:
            return z == top
        rule = z + 2 * groups * (k >= per // 2) * upper == (middle ^ s) + 2 * groups if k >= per // 2 else None
        if s != lead:
            return rule
        ends = z + upper == top + 1
        return ends if rule is None else jnp.logical_or(rule, ends)

    for s in range(groups - 1, -1, -1):
        for k in range(per):
            if s or k:
                rule = later(s, k)
                send_now = functools.partial(greet, barrier, s, k)
                send_now() if rule is None else pl.when(jnp.logical_not(rule))(send_now)

    def equal(a, b):
        return (a == b).astype(jnp.int32)

    def enter():
        left_out = per * equal(z, middle) + per // 2 * equal(z, middle - 1)
        pl.semaphore_wait(barrier, n - 1 - left_out - (groups - 1) * (per // 2) * equal(z + groups * upper, middle))

    def announce():
        for s in range(groups):
            for k in range(per):
                rule = later(s, k) if s or k else None
                if rule is not None:
                    pl.when(rule)(functools.partial(greet, notice, s, k))

    free = [left_sem.at[0], stem_sem.at[0], left_sem.at[1], stem_sem.at[1]]
    branch_copies = {
        s: pltpu.make_async_copy(branch_ref.at[:, :, :, column(s)], branch[s], sem)
        for s, sem in zip(sequence[1:] + [lead], free)}
    order_copy.wait()
    o0, o1, o2, o3 = (order[k] for k in range(4))

    def left_rows(s):
        return jnp.concatenate([branch[s][o0, part].T for part in range(2)], axis=0)

    def first_rows(s):
        return complex_rows(left_rows(s), xh, xl)

    def partner(s, i):
        if s == lead:
            return i
        if s != last:
            return flip(q, i, per)
        column = upper if i >= per // 2 else 1 - upper
        return column * (per // 2) + (per - 1 - i) % (per // 2)

    def hop(s, i, h=None):
        j = partner(s, i)
        where = () if h is None else (slice(None), slice(None), halves[h])
        return pltpu.make_async_remote_copy(
            src_ref=sent.at[(s * per + j, *where)], dst_ref=got.at[(s, q, *where)], send_sem=send_sem,
            recv_sem=recv_sem.at[groups - 1 + h if s == last else s - (s > last)],
            device_id={"mode": flip(z, s, groups) * per + j}, device_id_type=MESH)

    def await_bytes(place, sem):
        pltpu.make_async_copy(place, place, sem).wait()

    def own(s):
        return pltpu.make_async_copy(sent.at[s * per + q], got.at[s, q], recv_sem.at[s - (s > last)])

    def send(s, real, imag, which=range(per)):
        for place, j in enumerate(which):
            sent[s * per + j, 0] = real[place * rows:(place + 1) * rows]
            sent[s * per + j, 1] = imag[place * rows:(place + 1) * rows]
        for h in range(2) if s == last else [None]:
            for i in which:
                own(s).start() if s == 0 and i == 0 else hop(s, i, h).start()

    highs, lows = [], []
    parcels = [range(1), range(1, per)]
    cut = 2 * rows
    by = [None, None]

    def send_lead(by, which, h=None, admit=None):
        m = by[0].shape[0] // 2
        side = slice(None) if h is None else slice(h * (bw // 2), (h + 1) * (bw // 2))
        for part, value in enumerate((by[0][:m] - by[1][m:], by[1][:m] + by[0][m:])):
            for place, j in enumerate(which):
                sent[lead * per + j, part, :, side] = value[place * rows:(place + 1) * rows]
        for j in which:
            if admit and j == per // 2:
                admit()
            hop(lead, j, h).start()

    left_side, right_side = slice(0, bw // 2), slice(bw // 2, bw)
    for k, half in enumerate(halves):
        left_copies[k].wait()
        high, low = split(jnp.concatenate([
            left[k][o0, part].T[which[0] * rows:(which[-1] + 1) * rows] for which in parcels for part in range(2)], axis=0))
        highs.append(high)
        lows.append(low)
        stem_copies[k].wait()
        for part in range(2):
            xh[part, half, left_side], xl[part, half, left_side] = split(stem[part, half, left_side])
            add = dot3(high[:cut], low[:cut], xh[part, half, left_side], xl[part, half, left_side])
            by[part] = add if k == 0 else by[part] + add
    enter()
    send_lead(by, parcels[0], 0)
    announce()
    side_copy.wait()
    for s in sequence[1:] + [lead]:
        branch_copies[s].start()
    for part in range(2):
        xh[part, :, right_side], xl[part, :, right_side] = split(stem[part, :, right_side])
    high, low = (jnp.concatenate([piece[:cut] for piece in pieces], axis=1) for pieces in (highs, lows))
    send_lead([dot3(high, low, xh[part, :, right_side], xl[part, :, right_side]) for part in range(2)], parcels[0], 1)
    high, low = (jnp.concatenate([piece[cut:] for piece in pieces], axis=1) for pieces in (highs, lows))
    rest = [dot3(high, low, xh[part], xl[part]) for part in range(2)]
    def admit():
        pl.when(z == middle - 1)(lambda: pl.semaphore_wait(notice, per // 2))
        pl.when(z + groups * upper == middle)(lambda: pl.semaphore_wait(notice, per + (groups - 1) * (per // 2)))

    send_lead(rest, parcels[1], None, admit)
    for s in early[1:]:
        branch_copies[s].wait()
        if s == near:
            pl.when(z + groups * upper == middle + groups)(lambda: pl.semaphore_wait(notice, per))
        send(s, *first_rows(s))
    for s in sequence[len(early):] + [lead]:
        branch_copies[s].wait()

    for s in range(groups):
        for part in range(2):
            bh[part, :, column(s)], bl[part, :, column(s)] = split(branch[s][o1, part])
            dh[part, :, column(s)], dl[part, :, column(s)] = split(branch[s][o3, part])

    def both(i, carry):
        at = pl.ds(pl.multiple_of(i * LANES, LANES), LANES)
        high = jnp.concatenate([bh[0, at], bh[1, at]], axis=0)
        low = jnp.concatenate([bl[0, at], bl[1, at]], axis=0)
        by_real = dot3(high, low, dh[0], dl[0])
        by_imag = dot3(high, low, dh[1], dl[1])
        wh[0, at], wl[0, at] = split(by_real[:LANES] - by_imag[LANES:])
        wh[1, at], wl[1, at] = split(by_imag[:LANES] + by_real[LANES:])
        return carry

    lax.fori_loop(0, bw // LANES, both, 0)

    for s in sequence[len(early):]:
        real, imag = first_rows(s)
        send(s, *complex_rows(jnp.concatenate([real, imag], axis=0), wh, wl))

    for s in range(groups):
        high_ref, low_ref = (last_high, last_low) if s == last else (lch.at[s], lcl.at[s])
        for t in range(groups):
            real, imag = (split(branch[t][o2, part, column(s), :].T) for part in range(2))
            top = column(t)
            low_half = pl.ds(pl.multiple_of(bw + flip(z, t, groups) * LANES, LANES), LANES)
            for ref, r, i in ((high_ref, real[0], imag[0]), (low_ref, real[1], imag[1])):
                ref[top, :LANES] = r
                ref[top, LANES:] = -i
                ref[low_half, :LANES] = i
                ref[low_half, LANES:] = r

    arrivals = [0] + [s for s in early if s != groups // 2] + [groups // 2] + [s for s in sequence[len(early):] if s]
    tile = 2 * LANES

    def arrived(s, side):
        return jnp.concatenate([got[s, j, part, :, side] for part in range(2) for j in range(per)], axis=0)

    for index, s in enumerate(arrivals):
        if s == last:
            await_bytes(got.at[last, :, :, :, halves[0]], recv_sem.at[groups - 1])
            side = slice(0, bw // 2)
        else:
            await_bytes(got.at[s], recv_sem.at[s - (s > last)])
            side = slice(0, bw)
        right = arrived(s, side)
        if s in early:
            right = jnp.concatenate(complex_rows(right, wh, wl), axis=0)
        right_high, right_low = split(right)
        high_ref, low_ref = (last_high, last_low) if s == last else (lch.at[s], lcl.at[s])
        for i in range(2 * bw // tile):
            at = slice(i * tile, (i + 1) * tile)
            part, row = divmod(i * tile, bw)
            place = (part, slice(row, row + tile), side)
            add = dot3(high_ref[at], low_ref[at], right_high, right_low)
            out_ref[place] = add if index == 0 else out_ref[place] + add
    await_bytes(sent.at[pl.ds(0, n - 1)], send_sem)
    await_bytes(got.at[last, :, :, :, halves[1]], recv_sem.at[groups])
    tail_high[...], tail_low[...] = split(arrived(last, slice(bw // 2, bw)))


def finish(acc_ref, high_ref, low_ref, right_high, right_low, out_ref, tiles, sem):
    count, tile, half = tiles.shape
    ready = pltpu.make_async_copy(acc_ref.at[:, :, pl.ds(0, half)], out_ref.at[:, :, pl.ds(0, half)], sem.at[0])
    ready.start()
    right = right_high[...], right_low[...]
    for i in range(count):
        part, row = divmod(i * tile, 2 * half)
        at = slice(i * tile, (i + 1) * tile)
        tiles[i] = acc_ref[part, row:row + tile, half:] + dot3(high_ref[at], low_ref[at], *right)
        pltpu.make_async_copy(tiles.at[i], out_ref.at[part, pl.ds(row, tile), pl.ds(half, half)], sem.at[1]).start()
    ready.wait()
    pltpu.make_async_copy(tiles, tiles, sem.at[1]).wait()


def fused(n, stem_tensor, branch_tensors, branch_order):
    bw = stem_tensor.shape[-1]
    rows = bw // n
    per = LANES // rows
    groups = n // per
    square = pltpu.VMEM((2, bw, bw), BF16)
    hbm = functools.partial(pltpu.with_memory_space_constraint, memory_space=pltpu.HBM)
    window = pltpu.VMEM((groups, 2 * bw, 2 * LANES), BF16)
    vmem = pl.BlockSpec(memory_space=pltpu.VMEM)
    tiles = 2 * bw // LANES
    partial = pl.pallas_call(
        functools.partial(kernel, n),
        out_shape=[
            jax.ShapeDtypeStruct((2, bw, bw), F32),
            *[jax.ShapeDtypeStruct((2 * bw, 2 * LANES), BF16)] * 2,
            *[jax.ShapeDtypeStruct((2 * LANES, bw // 2), BF16)] * 2,
        ],
        in_specs=[pl.BlockSpec(memory_space=pl.ANY)] * 3,
        out_specs=[vmem] * 5,
        scratch_shapes=[
            pltpu.VMEM((2, bw, bw), F32),
            *[square] * 8,
            window,
            window,
            pltpu.VMEM((n, 2, rows, bw), F32),
            pltpu.VMEM((groups, per, 2, rows, bw), F32),
            pltpu.SMEM(branch_order.shape, jnp.int32),
            pltpu.SemaphoreType.DMA,
            pltpu.SemaphoreType.DMA((2,)),
            pltpu.SemaphoreType.DMA((2,)),
            pltpu.SemaphoreType.DMA,
            pltpu.SemaphoreType.DMA,
            pltpu.SemaphoreType.DMA((groups + 1,)),
            pltpu.SemaphoreType.REGULAR,
            *[pltpu.VMEM((4, 2, bw // 2, LANES), F32)] * 2,
            *[pltpu.VMEM((4, 2, bw, LANES), F32)] * groups,
        ],
        compiler_params=pltpu.CompilerParams(collective_id=0, has_side_effects=True, vmem_limit_bytes=40 << 20),
    )(hbm(branch_order), hbm(stem_tensor.reshape(2, bw, bw)), hbm(branch_tensors))
    return pl.pallas_call(
        finish,
        out_shape=jax.ShapeDtypeStruct((2, bw, bw), F32),
        in_specs=[vmem] * 5,
        out_specs=pl.BlockSpec(memory_space=pl.ANY),
        scratch_shapes=[pltpu.VMEM((tiles, LANES, bw // 2), F32), pltpu.SemaphoreType.DMA((2,))],
        compiler_params=pltpu.CompilerParams(vmem_limit_bytes=8 << 20),
    )(*partial).reshape(stem_tensor.shape)


def complex_product(first, second, form):
    high = lax.Precision.HIGHEST
    real = jnp.einsum(form, first[0], second[0], precision=high) - jnp.einsum(form, first[1], second[1], precision=high)
    imag = jnp.einsum(form, first[0], second[1], precision=high) + jnp.einsum(form, first[1], second[0], precision=high)
    return jnp.stack([real, imag])


def plain(stem_tensor, branch_tensors, branch_order):
    field = stem_tensor[:, :, 0]
    chosen = [branch_tensors[branch_order[index]] for index in range(4)]
    field = complex_product(field, chosen[0], "sce,cd->sde")
    field = complex_product(field, chosen[1], "sce,ed->scd")
    moved = lax.all_to_all(field[:, :, None], "mode", split_axis=3, concat_axis=2, tiled=True)
    merged = moved.reshape(field.shape)
    merged = complex_product(merged, chosen[2], "sce,cd->sde")
    return complex_product(merged, chosen[3], "sce,ed->scd")[:, :, None]


def on_device(n, stem_tensor, branch_tensors, branch_order):
    _, stems, held, bw, _ = stem_tensor.shape
    rows = bw // n
    fits = stems == held == 1 and rows % 8 == 0 and 3 * rows <= LANES and n & (n - 1) == 0 and n * rows == bw
    if fits and bw % (4 * LANES) == 0:
        return fused(n, stem_tensor, branch_tensors, branch_order)
    return plain(stem_tensor, branch_tensors, branch_order)


def solution(mesh):
    return jax.shard_map(
        functools.partial(on_device, mesh.shape["mode"]),
        mesh=mesh,
        in_specs=(P(None, "cuts", "mode", None, None), P(), P()),
        out_specs=P(None, "cuts", "mode", None, None),
        check_vma=False,
    )
```

```python
import functools

import jax
import jax.numpy as jnp
from jax import lax
from jax.experimental import pallas as pl
from jax.experimental.pallas import tpu as pltpu
from jax.sharding import PartitionSpec as P

MESH = pl.DeviceIdType.MESH
LANES = 128
F32, BF16 = jnp.float32, jnp.bfloat16


def flip(value, mask, size):
    result, bit = 0, 1
    while bit < size:
        digit = lax.rem(lax.div(value, bit), 2)
        result = result + (1 - digit if (mask // bit) % 2 else digit) * bit
        bit *= 2
    return result


def split(value):
    high = value.astype(BF16)
    return high, (value - high.astype(F32)).astype(BF16)


def dot(a, b):
    return jnp.dot(a, b, preferred_element_type=F32)


def dot3(high, low, right_high, right_low):
    return dot(high, right_high) + (dot(high, right_low) + dot(low, right_high))


def complex_rows(rows, right_high, right_low):
    m = rows.shape[0] // 2
    high, low = split(rows)
    by_real = dot3(high, low, right_high[0], right_low[0])
    by_imag = dot3(high, low, right_high[1], right_low[1])
    return by_real[:m] - by_imag[m:], by_imag[:m] + by_real[m:]


def kernel(n, order_ref, stem_ref, branch_ref, out_ref, last_high, last_low, tail_high, tail_low, stem, xh, xl, bh, bl, dh, dl, wh, wl,
           lch, lcl, sent, got, order, order_sem, stem_sem, left_sem, side_sem, send_sem, recv_sem, notice, left_0, left_1, *branch):
    bw = stem.shape[1]
    rows = bw // n
    per = LANES // rows
    groups = n // per
    me = lax.axis_index("mode")
    z, q = lax.div(me, per), lax.rem(me, per)
    upper = lax.div(q, per // 2)
    sequence = [groups // 2] + [s for s in range(1, groups) if s != groups // 2] + [0]
    early = sequence[: groups // 2]
    lead, last = sequence[0], sequence[-2]

    def column(s):
        return pl.ds(pl.multiple_of(flip(z, s, groups) * LANES, LANES), LANES)

    order_copy = pltpu.make_async_copy(order_ref, order, order_sem)
    order_copy.start()
    halves = [pl.ds(h * (bw // 2), bw // 2) for h in range(2)]
    left = (left_0, left_1)
    left_copies = [pltpu.make_async_copy(
        branch_ref.at[:, :, half, column(lead)], left[h], left_sem.at[h]) for h, half in enumerate(halves)]
    stem_copies = [pltpu.make_async_copy(
        stem_ref.at[:, half, halves[0]], stem.at[:, half, halves[0]], stem_sem.at[k]) for k, half in enumerate(halves)]
    side_copy = pltpu.make_async_copy(stem_ref.at[:, :, halves[1]], stem.at[:, :, halves[1]], side_sem)
    for copy in (left_copies[0], stem_copies[0], left_copies[1], stem_copies[1], side_copy):
        copy.start()
    barrier = pltpu.get_barrier_semaphore()
    top, middle = groups - 1, groups // 2
    near = middle ^ top

    def greet(sem, s, k):
        pl.semaphore_signal(
            sem, inc=1, device_id={"mode": flip(z, s, groups) * per + flip(q, k, per)}, device_id_type=MESH)

    for s in range(groups - 1, -1, -1):
        for k in range(per):
            if s == near:
                pl.when(z != top)(functools.partial(greet, barrier, s, k))
            elif s == lead:
                pl.when(z + upper != top + 1)(functools.partial(greet, barrier, s, k))
            elif s or k:
                greet(barrier, s, k)

    def equal(a, b):
        return (a == b).astype(jnp.int32)

    def enter():
        pl.semaphore_wait(barrier, n - 1 - per * equal(z, middle) - per // 2 * equal(z, middle - 1))

    def announce():
        for k in range(per):
            pl.when(z == top)(functools.partial(greet, notice, near, k))
            pl.when(z + upper == top + 1)(functools.partial(greet, notice, lead, k))

    free = [left_sem.at[0], stem_sem.at[0], left_sem.at[1], stem_sem.at[1]]
    branch_copies = {
        s: pltpu.make_async_copy(branch_ref.at[:, :, :, column(s)], branch[s], sem)
        for s, sem in zip(sequence[1:] + [lead], free)}
    order_copy.wait()
    o0, o1, o2, o3 = (order[k] for k in range(4))

    def left_rows(s):
        return jnp.concatenate([branch[s][o0, part].T for part in range(2)], axis=0)

    def first_rows(s):
        return complex_rows(left_rows(s), xh, xl)

    def partner(s, i):
        if s == lead:
            return i
        if s != last:
            return flip(q, i, per)
        column = upper if i >= per // 2 else 1 - upper
        return column * (per // 2) + (per - 1 - i) % (per // 2)

    def hop(s, i, h=None):
        j = partner(s, i)
        where = () if h is None else (slice(None), slice(None), halves[h])
        return pltpu.make_async_remote_copy(
            src_ref=sent.at[(s * per + j, *where)], dst_ref=got.at[(s, q, *where)], send_sem=send_sem,
            recv_sem=recv_sem.at[1 + h if s == last else 0],
            device_id={"mode": flip(z, s, groups) * per + j}, device_id_type=MESH)

    def await_bytes(place, sem):
        pltpu.make_async_copy(place, place, sem).wait()

    def own(s):
        return pltpu.make_async_copy(sent.at[s * per + q], got.at[s, q], recv_sem.at[0])

    def send(s, real, imag, which=range(per)):
        for place, j in enumerate(which):
            sent[s * per + j, 0] = real[place * rows:(place + 1) * rows]
            sent[s * per + j, 1] = imag[place * rows:(place + 1) * rows]
        for h in range(2) if s == last else [None]:
            for i in which:
                own(s).start() if s == 0 and i == 0 else hop(s, i, h).start()

    highs, lows = [], []
    parcels = [range(per // 2), range(per // 2, per)]
    by = [None, None]

    def send_lead(by, which, h=None):
        m = by[0].shape[0] // 2
        side = slice(None) if h is None else slice(h * (bw // 2), (h + 1) * (bw // 2))
        for part, value in enumerate((by[0][:m] - by[1][m:], by[1][:m] + by[0][m:])):
            for place, j in enumerate(which):
                sent[lead * per + j, part, :, side] = value[place * rows:(place + 1) * rows]
        for j in which:
            hop(lead, j, h).start()

    left_side, right_side = slice(0, bw // 2), slice(bw // 2, bw)
    for k, half in enumerate(halves):
        left_copies[k].wait()
        high, low = split(jnp.concatenate([
            left[k][o0, part].T[which[0] * rows:(which[-1] + 1) * rows] for which in parcels for part in range(2)], axis=0))
        highs.append(high)
        lows.append(low)
        stem_copies[k].wait()
        for part in range(2):
            xh[part, half, left_side], xl[part, half, left_side] = split(stem[part, half, left_side])
            add = dot3(high[:LANES], low[:LANES], xh[part, half, left_side], xl[part, half, left_side])
            by[part] = add if k == 0 else by[part] + add
    enter()
    send_lead(by, parcels[0], 0)
    announce()
    side_copy.wait()
    for s in sequence[1:] + [lead]:
        branch_copies[s].start()
    for part in range(2):
        xh[part, :, right_side], xl[part, :, right_side] = split(stem[part, :, right_side])
    high, low = (jnp.concatenate([piece[:LANES] for piece in pieces], axis=1) for pieces in (highs, lows))
    send_lead([dot3(high, low, xh[part, :, right_side], xl[part, :, right_side]) for part in range(2)], parcels[0], 1)
    high, low = (jnp.concatenate([piece[LANES:] for piece in pieces], axis=1) for pieces in (highs, lows))
    rest = [dot3(high, low, xh[part], xl[part]) for part in range(2)]
    pl.when(z == middle - 1)(lambda: pl.semaphore_wait(notice, per // 2))
    send_lead(rest, parcels[1])
    for s in early[1:]:
        branch_copies[s].wait()
        if s == near:
            pl.when(z == middle)(lambda: pl.semaphore_wait(notice, per))
        send(s, *first_rows(s))
    for s in sequence[len(early):] + [lead]:
        branch_copies[s].wait()

    for s in range(groups):
        for part in range(2):
            bh[part, :, column(s)], bl[part, :, column(s)] = split(branch[s][o1, part])
            dh[part, :, column(s)], dl[part, :, column(s)] = split(branch[s][o3, part])

    def both(i, carry):
        at = pl.ds(pl.multiple_of(i * LANES, LANES), LANES)
        high = jnp.concatenate([bh[0, at], bh[1, at]], axis=0)
        low = jnp.concatenate([bl[0, at], bl[1, at]], axis=0)
        by_real = dot3(high, low, dh[0], dl[0])
        by_imag = dot3(high, low, dh[1], dl[1])
        wh[0, at], wl[0, at] = split(by_real[:LANES] - by_imag[LANES:])
        wh[1, at], wl[1, at] = split(by_imag[:LANES] + by_real[LANES:])
        return carry

    lax.fori_loop(0, bw // LANES, both, 0)

    for s in sequence[len(early):]:
        real, imag = first_rows(s)
        send(s, *complex_rows(jnp.concatenate([real, imag], axis=0), wh, wl))

    for s in range(groups):
        high_ref, low_ref = (last_high, last_low) if s == last else (lch.at[s], lcl.at[s])
        for t in range(groups):
            real, imag = (split(branch[t][o2, part, column(s), :].T) for part in range(2))
            top = column(t)
            low_half = pl.ds(pl.multiple_of(bw + flip(z, t, groups) * LANES, LANES), LANES)
            for ref, r, i in ((high_ref, real[0], imag[0]), (low_ref, real[1], imag[1])):
                ref[top, :LANES] = r
                ref[top, LANES:] = -i
                ref[low_half, :LANES] = i
                ref[low_half, LANES:] = r

    arrivals = [0] + [s for s in early if s != groups // 2] + [groups // 2] + [s for s in sequence[len(early):] if s]
    tile = 2 * LANES

    def arrived(s, side):
        return jnp.concatenate([got[s, j, part, :, side] for part in range(2) for j in range(per)], axis=0)

    for index, s in enumerate(arrivals):
        if s == last:
            await_bytes(got.at[last, :, :, :, halves[0]], recv_sem.at[1])
            side = slice(0, bw // 2)
        else:
            if index == 0:
                await_bytes(got.at[pl.ds(0, groups - 1)], recv_sem.at[0])
            side = slice(0, bw)
        right = arrived(s, side)
        if s in early:
            right = jnp.concatenate(complex_rows(right, wh, wl), axis=0)
        right_high, right_low = split(right)
        high_ref, low_ref = (last_high, last_low) if s == last else (lch.at[s], lcl.at[s])
        for i in range(2 * bw // tile):
            at = slice(i * tile, (i + 1) * tile)
            part, row = divmod(i * tile, bw)
            place = (part, slice(row, row + tile), side)
            add = dot3(high_ref[at], low_ref[at], right_high, right_low)
            out_ref[place] = add if index == 0 else out_ref[place] + add
    await_bytes(sent.at[pl.ds(0, n - 1)], send_sem)
    await_bytes(got.at[last, :, :, :, halves[1]], recv_sem.at[2])
    tail_high[...], tail_low[...] = split(arrived(last, slice(bw // 2, bw)))


def finish(acc_ref, high_ref, low_ref, right_high, right_low, out_ref, tiles, sem):
    count, tile, half = tiles.shape
    ready = pltpu.make_async_copy(acc_ref.at[:, :, pl.ds(0, half)], out_ref.at[:, :, pl.ds(0, half)], sem.at[0])
    ready.start()
    right = right_high[...], right_low[...]
    for i in range(count):
        part, row = divmod(i * tile, 2 * half)
        at = slice(i * tile, (i + 1) * tile)
        tiles[i] = acc_ref[part, row:row + tile, half:] + dot3(high_ref[at], low_ref[at], *right)
        pltpu.make_async_copy(tiles.at[i], out_ref.at[part, pl.ds(row, tile), pl.ds(half, half)], sem.at[1]).start()
    ready.wait()
    pltpu.make_async_copy(tiles, tiles, sem.at[1]).wait()


def fused(n, stem_tensor, branch_tensors, branch_order):
    bw = stem_tensor.shape[-1]
    rows = bw // n
    per = LANES // rows
    groups = n // per
    square = pltpu.VMEM((2, bw, bw), BF16)
    hbm = functools.partial(pltpu.with_memory_space_constraint, memory_space=pltpu.HBM)
    window = pltpu.VMEM((groups, 2 * bw, 2 * LANES), BF16)
    vmem = pl.BlockSpec(memory_space=pltpu.VMEM)
    tiles = 2 * bw // LANES
    partial = pl.pallas_call(
        functools.partial(kernel, n),
        out_shape=[
            jax.ShapeDtypeStruct((2, bw, bw), F32),
            *[jax.ShapeDtypeStruct((2 * bw, 2 * LANES), BF16)] * 2,
            *[jax.ShapeDtypeStruct((2 * LANES, bw // 2), BF16)] * 2,
        ],
        in_specs=[pl.BlockSpec(memory_space=pl.ANY)] * 3,
        out_specs=[vmem] * 5,
        scratch_shapes=[
            pltpu.VMEM((2, bw, bw), F32),
            *[square] * 8,
            window,
            window,
            pltpu.VMEM((n, 2, rows, bw), F32),
            pltpu.VMEM((groups, per, 2, rows, bw), F32),
            pltpu.SMEM(branch_order.shape, jnp.int32),
            pltpu.SemaphoreType.DMA,
            pltpu.SemaphoreType.DMA((2,)),
            pltpu.SemaphoreType.DMA((2,)),
            pltpu.SemaphoreType.DMA,
            pltpu.SemaphoreType.DMA,
            pltpu.SemaphoreType.DMA((3,)),
            pltpu.SemaphoreType.REGULAR,
            *[pltpu.VMEM((4, 2, bw // 2, LANES), F32)] * 2,
            *[pltpu.VMEM((4, 2, bw, LANES), F32)] * groups,
        ],
        compiler_params=pltpu.CompilerParams(collective_id=0, has_side_effects=True, vmem_limit_bytes=40 << 20),
    )(hbm(branch_order), hbm(stem_tensor.reshape(2, bw, bw)), hbm(branch_tensors))
    return pl.pallas_call(
        finish,
        out_shape=jax.ShapeDtypeStruct((2, bw, bw), F32),
        in_specs=[vmem] * 5,
        out_specs=pl.BlockSpec(memory_space=pl.ANY),
        scratch_shapes=[pltpu.VMEM((tiles, LANES, bw // 2), F32), pltpu.SemaphoreType.DMA((2,))],
        compiler_params=pltpu.CompilerParams(vmem_limit_bytes=8 << 20),
    )(*partial).reshape(stem_tensor.shape)


def complex_product(first, second, form):
    high = lax.Precision.HIGHEST
    real = jnp.einsum(form, first[0], second[0], precision=high) - jnp.einsum(form, first[1], second[1], precision=high)
    imag = jnp.einsum(form, first[0], second[1], precision=high) + jnp.einsum(form, first[1], second[0], precision=high)
    return jnp.stack([real, imag])


def plain(stem_tensor, branch_tensors, branch_order):
    field = stem_tensor[:, :, 0]
    chosen = [branch_tensors[branch_order[index]] for index in range(4)]
    field = complex_product(field, chosen[0], "sce,cd->sde")
    field = complex_product(field, chosen[1], "sce,ed->scd")
    moved = lax.all_to_all(field[:, :, None], "mode", split_axis=3, concat_axis=2, tiled=True)
    merged = moved.reshape(field.shape)
    merged = complex_product(merged, chosen[2], "sce,cd->sde")
    return complex_product(merged, chosen[3], "sce,ed->scd")[:, :, None]


def on_device(n, stem_tensor, branch_tensors, branch_order):
    _, stems, held, bw, _ = stem_tensor.shape
    rows = bw // n
    fits = stems == held == 1 and rows % 8 == 0 and 3 * rows <= LANES and n & (n - 1) == 0 and n * rows == bw
    if fits and bw % (4 * LANES) == 0:
        return fused(n, stem_tensor, branch_tensors, branch_order)
    return plain(stem_tensor, branch_tensors, branch_order)


def solution(mesh):
    return jax.shard_map(
        functools.partial(on_device, mesh.shape["mode"]),
        mesh=mesh,
        in_specs=(P(None, "cuts", "mode", None, None), P(), P()),
        out_specs=P(None, "cuts", "mode", None, None),
        check_vma=False,
    )
```
